256 devices in a mesh: bulk: 16 (over z_lo, x), tp: 16 (over z_hi, y, core).
Axes of the slice: x: 4, y: 4, z: 8 (z_hi: 2, z_lo: 4; z = z_hi * 4 + z_lo), core: 2. Of those that a mesh axis runs over, the one named last changes fastest.
Arguments:
- queries: bfloat16 [16384, 8192], P('bulk', 'tp'), may hold values from -40 to 40, as said below
- comp_keys: bfloat16 [16384, 1024], P(('bulk', 'tp')), may hold values from -8 to 8
- comp_values: bfloat16 [16384, 1024], P(('bulk', 'tp')), may hold values from -6 to 6
- prefix_keys: bfloat16 [16, 2048, 1024], P('bulk', 'tp'), may hold values from -10 to 10
- prefix_values: bfloat16 [16, 2048, 1024], P('bulk', 'tp'), may hold values from -6 to 6
- lengths: int32 [16, 16], P('bulk'), may hold values from 1 to 64, as said below
- routing: int32 [16, 64], P('bulk'), may hold values from 0 to 15, as said below
- residual: bfloat16 [16384, 8192], P('bulk', 'tp'), may hold values from -6 to 6
- out_weight: bfloat16 [8192, 8192], P('tp'), may hold values from -0.09375 to 0.09375
Outputs:
- mixed: bfloat16 [8192, 8192], P('bulk', 'tp')
The draws below stay inside these ranges and needn't reach their ends.
Inputs may be any that keep to these rules, and one draw needn't show every extreme that they name: queries are of order one except on some rows of the hidden draw. `lengths`: for every prompt, the sum over its completions of ceil(length / 8) is at most 64, and it equals 64 for some prompt in every draw. `routing`: in every row, each index of bulk appears exactly 4 times.
All inputs are finite; a program needn't handle non-finite values.
Results may differ from the reference program's by a relative error of at most 0.009.
Values may be sent and summed in bfloat16 or wider, within the bound.
A program may use at most 128 MiB of HBM per device.

```python
import math
import jax
import jax.numpy as jnp
from jax import lax

D = 8192
HEADS = 64
KVH = 8
HD = 128
PLEN = 2048
CMAX = 64
GROUP = 16
BLK = 8
SLOTS = 64
PROMPTS = 16
HOME = 1024
ROWS = 16384
CAP = 4
N_BULK = 16
N_TP = 16


def prefix_base(key):
    values_raw = jax.random.normal(jax.random.fold_in(key, 101), (PROMPTS, PLEN, KVH * HD), jnp.float32)
    return jnp.clip(values_raw, -4.0, 4.0)


def draw_prefix_keys(key, part):
    values_raw = prefix_base(key)
    return values_raw.astype(jnp.bfloat16)


def draw_queries(key, part):
    values_raw = jax.random.normal(jax.random.fold_in(key, 202), (ROWS, HEADS * HD), jnp.float32)
    values_raw = 2.5 * jnp.clip(values_raw, -4.0, 4.0)
    return values_raw.astype(jnp.bfloat16)


def draw_lengths(key, part):
    per_comp = CMAX // BLK
    base_key = jax.random.fold_in(key, 303)
    extra_room = SLOTS - GROUP
    picks = jax.random.randint(jax.random.fold_in(base_key, 1), (PROMPTS,), 0, extra_room + 1)
    totals = picks * picks // max(extra_room, 1)
    fullest = jax.random.randint(jax.random.fold_in(base_key, 2), (), 0, PROMPTS)
    prompt_ids = jnp.arange(PROMPTS, dtype=jnp.int32)
    totals = jnp.where(prompt_ids == fullest, extra_room, totals)
    favoured = jax.random.randint(jax.random.fold_in(base_key, 5), (), 0, GROUP)
    spare = GROUP * (per_comp - 1)
    prompt_keys = jax.random.split(jax.random.fold_in(base_key, 3), PROMPTS)
    ranking = jax.vmap(lambda single: jax.random.permutation(single, spare))(prompt_keys).astype(jnp.int32)
    owner = jnp.arange(spare, dtype=jnp.int32) // (per_comp - 1)
    boosted = (prompt_ids[:, None] == fullest) & (owner[None, :] == favoured)
    order_key = ranking - jnp.where(boosted, spare, 0).astype(jnp.int32)
    position = jnp.argsort(jnp.argsort(order_key, axis=1), axis=1).astype(jnp.int32)
    chosen = position < totals[:, None]
    members = chosen[:, :, None] & (owner[None, :, None] == jnp.arange(GROUP, dtype=jnp.int32)[None, None, :])
    extra = jnp.sum(members.astype(jnp.int32), axis=1)
    tail_rows = jax.random.randint(jax.random.fold_in(base_key, 4), (PROMPTS, GROUP), 1, BLK + 1)
    full_one = (prompt_ids[:, None] == fullest) & (jnp.arange(GROUP, dtype=jnp.int32)[None, :] == favoured)
    tail_rows = jnp.where(full_one, BLK, tail_rows)
    return (extra * BLK + tail_rows).astype(jnp.int32)


def draw_routing(key, part):
    prompt_keys = jax.random.split(jax.random.fold_in(key, 404), PROMPTS)
    shuffled = jax.vmap(lambda single: jax.random.permutation(single, SLOTS))(prompt_keys)
    return (shuffled // CAP).astype(jnp.int32)


def with_spikes(array, key, source, target, parts, factor):
    owner, partner = [(jnp.arange(array.shape[dim]) // (array.shape[dim] // parts)).reshape([-1 if axis == dim else 1 for axis in range(array.ndim)]) for dim in (source, target)]
    chosen = jax.random.permutation(key, parts)[partner]
    strong = (owner == chosen) | (owner == (partner + parts // 2) % parts)
    return jnp.where(strong, factor * array, array)


def block_scale(rng, dims, shards, smallest, largest):
    gain = 1.0
    for dim, shards_of in shards:
        heights = jax.random.uniform(jax.random.fold_in(jax.random.fold_in(rng, 6), dim), (shards_of,), jnp.float32, smallest / len(shards), largest / len(shards))
        gain = gain * jnp.repeat(jnp.exp(heights), dims[dim] // shards_of).reshape((-1,) + (1,) * (len(dims) - 1 - dim))
    return gain


def gaussian(stream_key, extent, spread, most, pieces=(), kind=jnp.bfloat16):
    drawn = jax.random.normal(stream_key, extent, jnp.float32) * spread
    if len(pieces) > 0:
        drawn = block_scale(stream_key, extent, pieces, -0.22, 0.18) * drawn
    return jnp.clip(drawn, min=-most, max=most).astype(kind)


def bell_draw_with(rng, shape, scale, limit, shards, heavy, kind=jnp.bfloat16):
    array = scale * jax.random.normal(rng, shape, jnp.float32)
    if shards:
        array = array * block_scale(rng, shape, shards, -0.22, 0.18)
    return jnp.clip(with_spikes(array, jax.random.fold_in(rng, 3), *heavy), -limit, limit).astype(kind)


def setup_inputs(seed: int = 0) -> dict:
    arg_keys = jax.random.split(jax.random.key(seed), 10)
    return {
        "queries": draw_queries(jax.random.fold_in(arg_keys[9], 71), 0),
        "comp_keys": gaussian(arg_keys[1], (ROWS, KVH * HD), 1.4, 8.0, ((0, 256),)),
        "comp_values": gaussian(arg_keys[2], (ROWS, KVH * HD), 1.0, 6.0, ((0, 256),)),
        "prefix_keys": draw_prefix_keys(jax.random.fold_in(arg_keys[9], 71), 0),
        "prefix_values": gaussian(arg_keys[4], (PROMPTS, PLEN, KVH * HD), 1.0, 6.0, ((0, 16), (1, 16))),
        "lengths": draw_lengths(jax.random.fold_in(arg_keys[9], 71), 0),
        "routing": draw_routing(jax.random.fold_in(arg_keys[9], 71), 0),
        "residual": gaussian(arg_keys[7], (ROWS, D), 1.0, 6.0, ((0, 16), (1, 16))),
        "out_weight": bell_draw_with(arg_keys[8], (HEADS * HD, D), (HEADS * HD) ** -0.5, 0.09375, ((0, 16),), (0, 1, 16, 2.0)),
    }


def tables(lens_row, route_row, per_pair):
    per_comp = CMAX // BLK
    counts = ((lens_row + BLK - 1) // BLK).astype(jnp.int32)
    inner = jnp.arange(per_comp, dtype=jnp.int32)
    live_flags = (inner[None, :] < counts[:, None]).reshape(-1).astype(jnp.int32)
    live_rank = (jnp.cumsum(live_flags) - 1).astype(jnp.int32)
    block_total = live_flags.shape[0]
    slot_order = jnp.arange(SLOTS, dtype=jnp.int32)
    rank_hits = (live_rank[:, None] == slot_order[None, :]) & (live_flags[:, None] == 1)
    block_ids = jnp.arange(block_total, dtype=jnp.int32)
    block_of = lax.optimization_barrier(jnp.sum(jnp.where(rank_hits, block_ids[:, None], 0), axis=0)).astype(jnp.int32)
    slot_used = jnp.any(rank_hits, axis=0)
    same_dest = route_row[:, None] == route_row[None, :]
    earlier = slot_order[None, :] < slot_order[:, None]
    slot_place = (route_row * per_pair + lax.optimization_barrier(jnp.sum(same_dest & earlier, axis=1))).astype(jnp.int32)
    place_hits = slot_place[None, :] == slot_order[:, None]
    block_for = lax.optimization_barrier(jnp.sum(jnp.where(place_hits, block_of[None, :], 0), axis=1)).astype(jnp.int32)
    live_for = jnp.any(place_hits & slot_used[None, :], axis=1)
    return (block_for, live_for)

def attend(query_blk, key_own, value_own, key_pre, value_pre, lens_blk):
    inv_root = 1.0 / math.sqrt(query_blk.shape[-1])
    query_f = query_blk.astype(jnp.float32)
    score_pre = jnp.einsum('bckqh,pkh->bckqp', query_f, key_pre.astype(jnp.float32)) * inv_root
    score_own = jnp.einsum('bckqh,bekh->bckqe', query_f, key_own.astype(jnp.float32)) * inv_root
    positions = jnp.arange(query_blk.shape[1], dtype=jnp.int32)
    causal = positions[None, :] <= positions[:, None]
    score_own = jnp.where(causal[None, :, None, None, :], score_own, jnp.float32(-1e+30))
    top_score = jnp.maximum(lax.optimization_barrier(jnp.max(score_pre, axis=-1)), lax.optimization_barrier(jnp.max(score_own, axis=-1)))
    expo_pre = jnp.exp(score_pre - top_score[..., None])
    expo_own = jnp.exp(score_own - top_score[..., None])
    total = lax.optimization_barrier(jnp.sum(expo_pre, axis=-1)) + lax.optimization_barrier(jnp.sum(expo_own, axis=-1))
    weight_pre = lax.optimization_barrier(expo_pre.astype(jnp.bfloat16)).astype(jnp.float32)
    weight_own = lax.optimization_barrier(expo_own.astype(jnp.bfloat16)).astype(jnp.float32)
    summed = jnp.einsum('bckqp,pkh->bckqh', weight_pre, value_pre.astype(jnp.float32))
    summed = summed + jnp.einsum('bckqe,bekh->bckqh', weight_own, value_own.astype(jnp.float32))
    result = summed / total[..., None]
    valid = positions[None, :] < lens_blk[:, None]
    result = jnp.where(valid[:, :, None, None, None], result, jnp.float32(0.0))
    return result.astype(jnp.bfloat16)

def reference(queries, comp_keys, comp_values, prefix_keys, prefix_values, lengths, routing, residual, out_weight):
    group_size = HEADS // KVH
    per_pair = SLOTS // N_BULK
    block_total = HOME // BLK
    width_loc = HEADS * HD // N_TP
    query_all = queries.reshape(PROMPTS, GROUP, CMAX, KVH, group_size, HD)
    keys_all = comp_keys.reshape(PROMPTS, GROUP, CMAX, KVH, HD)
    values_all = comp_values.reshape(PROMPTS, GROUP, CMAX, KVH, HD)
    prekeys_all = prefix_keys.reshape(PROMPTS, PLEN, KVH, HD)
    prevalues_all = prefix_values.reshape(PROMPTS, PLEN, KVH, HD)
    resid_all = residual.reshape(PROMPTS, HOME, D)
    weight_parts = out_weight.reshape(N_TP, width_loc, D)

    def one_prompt(bundle):
        query_p, keys_p, values_p, prekeys_p, prevalues_p, lens_p, route_p, resid_p = bundle

        def one_completion(inner_bundle):
            query_c, keys_c, values_c, lens_c = inner_bundle
            return attend(query_c[None], keys_c[None], values_c[None], prekeys_p, prevalues_p, lens_c[None])[0]
        context = lax.map(one_completion, (query_p, keys_p, values_p, lens_p))
        context = context.reshape(HOME, HEADS * HD)
        summed = jnp.zeros((HOME, D), jnp.float32)
        for shard_index in range(N_TP):
            piece = jnp.dot(context[:, shard_index * width_loc:(shard_index + 1) * width_loc], weight_parts[shard_index], preferred_element_type=jnp.float32)
            summed = summed + lax.optimization_barrier(piece.astype(jnp.bfloat16)).astype(jnp.float32)
        row_ids = jnp.arange(HOME, dtype=jnp.int32)
        row_valid = row_ids % CMAX < lens_p[row_ids // CMAX]
        finished = jnp.where(row_valid[:, None], resid_p.astype(jnp.float32) + summed, jnp.float32(0.0)).astype(jnp.bfloat16)
        block_for, live_for = tables(lens_p, route_p, per_pair)
        picked = jnp.take(finished.reshape(block_total, BLK, D), block_for, axis=0)
        return jnp.where(live_for[:, None, None], picked, jnp.zeros((), jnp.bfloat16))
    sent = lax.map(one_prompt, (query_all, keys_all, values_all, prekeys_all, prevalues_all, lengths, routing, resid_all))
    sent = sent.reshape(PROMPTS, N_BULK, per_pair, BLK, D)
    sent = jnp.transpose(sent, (1, 0, 2, 3, 4))
    return sent.reshape(N_BULK * SLOTS * BLK, D)
```

```python
import math

import jax
import jax.numpy as jnp
from jax import lax
from jax.experimental import pallas as pl
from jax.experimental.pallas import tpu as pltpu
from jax.sharding import PartitionSpec as P

HD = 128
BLK = 8
NX, NY, NZL, NZH, NC = 4, 4, 4, 2, 2
NK = NX
CR = 128
LH = 4
FE = 512
SCALE = math.log2(math.e) / math.sqrt(HD)
F32, BF16 = jnp.float32, jnp.bfloat16
MESH = pl.DeviceIdType.MESH
NT = (((1,), (1,)), ((), ()))


def position():
    b, t = lax.axis_index("bulk"), lax.axis_index("tp")
    x, zl = lax.rem(b, NX), lax.div(b, NX)
    c, y, zh = lax.rem(t, NC), lax.rem(lax.div(t, NC), NY), lax.div(t, NC * NY)
    return x, zl, c, y, zh


def tables_kernel(lens, route, blk, nval, count):
    x, zl, _, _, _ = position()

    def clear(p, carry):
        blk[p] = 0
        nval[p] = 0
        return carry

    lax.fori_loop(0, 64, clear, 0)

    def clear_count(d, carry):
        count[d] = 0
        return carry

    lax.fori_loop(0, 16, clear_count, 0)

    def completion(i, j):
        size = lens[0, i]
        blocks = lax.div(size + BLK - 1, BLK)

        def block(n, carry):
            d = route[0, j + n]
            seen = count[d]
            count[d] = seen + 1
            k = lax.rem(lax.rem(d, NX) - x + 2 * NX - 1, NX)
            dz = lax.rem(lax.div(d, NX) - zl + NZL, NZL)
            p = (k * NZL + dz) * 4 + seen
            blk[p] = i * 8 + n
            nval[p] = jnp.minimum(size - n * BLK, BLK)
            return carry

        lax.fori_loop(0, blocks, block, 0)
        return j + blocks

    lax.fori_loop(0, 16, completion, 0)


def main_kernel(
    blk, nval, q, ck, cv, pk, pv, res, w, out,
    kv, wbuf, qv, rv, qf, rf, oown, mown, lown, scores, qc, oc, mc, lc, vc, rc,
    ctx, d2s, d2r, bs, br, ds, rx,
    q_sem, r_sem, kv_loc, kv_send, kv_recv, fw_send, fw_recv, w_loc, w_send, w_recv,
    c_send, c_recv, d2_send, d2_recv, b_send, b_recv, x_send, x_recv,
):
    x, zl, c, y, zh = position()
    oth = 1 - c
    bulk = zl * NX + x

    def bulk_at(dx, dz):
        return lax.rem(zl + dz, NZL) * NX + lax.rem(x + dx, NX)

    def tp_at(dzh, dy, core):
        return (lax.rem(zh + dzh, NZH) * NY + lax.rem(y + dy, NY)) * NC + core

    def remote(src, dst, send, recv, where):
        return pltpu.make_async_remote_copy(
            src_ref=src, dst_ref=dst, send_sem=send, recv_sem=recv, device_id=where, device_id_type=MESH
        )

    q_copy = pltpu.make_async_copy(q, qv, q_sem)
    r_copy = pltpu.make_async_copy(res, rv, r_sem)
    q_copy.start()
    r_copy.start()

    barrier = pltpu.get_barrier_semaphore()
    peers = [(bulk, tp_at(dzh, dy, c)) for dzh in range(NZH) for dy in range(NY) if dzh or dy]
    peers += [(bulk, tp_at(0, 0, oth))]
    peers += [
        (bulk_at(dx, dz), tp_at(dzh, 0, c))
        for dx in range(NX)
        for dz in range(NZL)
        for dzh in range(NZH)
        if dx or dz
    ]
    for where in peers:
        pl.semaphore_signal(barrier, inc=1, device_id=where, device_id_type=MESH)
    pl.semaphore_wait(barrier, len(peers))

    parts = (
        (pk.at[0], 0, 128),
        (pv.at[0], 128, 128),
        (ck, 256, 64),
        (cv, 320, 64),
    )

    def kv_copies(j):
        dzh, dy = j // NY, j % NY
        head = pl.multiple_of((lax.rem(zh + dzh, NZH) * NY + lax.rem(y + dy, NY)) * HD, HD)
        made = []
        for n, (src, at, rows) in enumerate(parts):
            s = src.at[:, pl.ds(head, HD)]
            d = kv.at[j, c, pl.ds(at, rows), :]
            if j == 0:
                made.append(pltpu.make_async_copy(s, d, kv_loc.at[n]))
            else:
                made.append(remote(s, d, kv_send.at[j, n], kv_recv.at[j, n], (bulk, tp_at(dzh, dy, c))))
        return made

    for j in (6, 5, 7, 4, 2, 1, 3, 0):
        for copy in kv_copies(j):
            copy.start()

    def w_copies(n):
        here = pltpu.make_async_copy(
            w.at[:, pl.ds(pl.multiple_of((2 * n + c) * FE, FE), FE)], wbuf.at[c, n], w_loc.at[n]
        )
        away = remote(
            w.at[:, pl.ds(pl.multiple_of((2 * n + oth) * FE, FE), FE)],
            wbuf.at[c, n],
            w_send.at[n],
            w_recv.at[n],
            (bulk, tp_at(0, 0, oth)),
        )
        return here, away

    for n in range(8):
        for copy in w_copies(n):
            copy.start()

    q_copy.wait()
    r_copy.wait()

    def widen(i, carry):
        rows = pl.ds(pl.multiple_of(i * 64, 64), 64)
        at = pl.ds(i * 8, 8)
        qf[at] = qv[rows, :].astype(F32).reshape(8, 8, FE)
        rf[at] = rv[rows, :].astype(F32).reshape(8, 8, FE)
        return carry

    lax.fori_loop(0, 16, widen, 0)

    def own_part(j, core):
        dzh, dy = lax.div(j, NY), lax.rem(j, NY)
        i = (lax.rem(zh + NZH - dzh, NZH) * NY + lax.rem(y + NY - dy, NY)) * NC + core
        rows = pl.ds(pl.multiple_of(i * 64, 64), 64)
        at = pl.ds(i * 8, 8)
        qs = jnp.concatenate([qv[rows, h * HD : (h + 1) * HD] for h in range(LH)], axis=0)
        s = lax.dot_general(qs, kv[j, core, 256:320, :], NT, preferred_element_type=F32) * SCALE
        row = lax.broadcasted_iota(jnp.int32, s.shape, 0) & 63
        col = lax.broadcasted_iota(jnp.int32, s.shape, 1)
        s = jnp.where(col <= row, s, -1e30)
        m = jnp.max(s, axis=1, keepdims=True)
        e = jnp.exp2(s - m)
        total = jnp.sum(e, axis=1, keepdims=True)
        o = jnp.dot(e.astype(BF16), kv[j, core, 320:384, :], preferred_element_type=F32)
        m, total = jnp.broadcast_to(m, o.shape), jnp.broadcast_to(total, o.shape)
        for h in range(LH):
            cols = slice(h * HD, (h + 1) * HD)
            part = slice(h * 64, (h + 1) * 64)
            oown[at, :, cols] = o[part].reshape(8, 8, HD)
            mown[at, :, cols] = m[part].reshape(8, 8, HD)
            lown[at, :, cols] = total[part].reshape(8, 8, HD)

    def forward(j):
        slot = kv.at[j, c]
        return remote(slot, slot, fw_send.at[j], fw_recv.at[j], (bulk, tp_at(0, 0, oth)))

    def from_sibling(j):
        slot = kv.at[j, oth]
        return remote(slot, slot, fw_send.at[j], fw_recv.at[j], (bulk, tp_at(0, 0, oth)))

    for j in (0, 1, 3, 2, 4, 5, 7, 6):
        for copy in kv_copies(j):
            if j == 0:
                copy.wait()
            else:
                copy.wait_recv()
        forward(j).start()
        own_part(j, c)

    def second(j, carry):
        from_sibling(j).wait_recv()
        own_part(j, oth)
        return carry

    lax.fori_loop(0, 8, second, 0)


    def attend(k):
        def gather(i, carry):
            b = blk[k * 16 + i]
            n = nval[k * 16 + i]
            at = pl.ds(pl.multiple_of(i * 8, 8), 8)
            qb, ob, mb, lb = qf[b], oown[b], mown[b], lown[b]
            for h in range(LH):
                cols = slice(h * HD, (h + 1) * HD)
                qc[h, at, :] = qb[:, cols]
                oc[h, at, :] = ob[:, cols]
                mc[h, at, :] = mb[:, cols]
                lc[h, at, :] = lb[:, cols]
            vc[at, :] = (lax.broadcasted_iota(jnp.int32, (8, HD), 0) < n).astype(F32)
            return carry

        lax.fori_loop(0, 16, gather, 0)

        for u in range(2):
            two = slice(2 * u, 2 * u + 2)
            qb = qc[two].reshape(2 * CR, HD).astype(BF16)
            top = None
            for j in range(8):
                s = lax.dot_general(
                    qb, kv[j, :, 0:128, :].reshape(256, HD), NT, preferred_element_type=F32
                )
                scores[j] = s
                both = jnp.maximum(s[:, :HD], s[:, HD:])
                top = both if top is None else jnp.maximum(top, both)
            m_own = mc[two].reshape(2 * CR, HD)
            m = jnp.maximum(jnp.max(top, axis=1, keepdims=True) * SCALE, m_own)
            wide = jnp.concatenate([m, m], axis=1)
            acc = jnp.zeros((2 * CR, HD), F32)
            sums = jnp.zeros((2 * CR, HD), F32)
            for j in range(8):
                e = jnp.exp2(scores[j] * SCALE - wide)
                sums = sums + (e[:, :HD] + e[:, HD:])
                acc = acc + jnp.dot(
                    e.astype(BF16), kv[j, :, 128:256, :].reshape(256, HD), preferred_element_type=F32
                )
            a = jnp.exp2(m_own - m)
            total = jnp.sum(sums, axis=1, keepdims=True) + a * lc[two].reshape(2 * CR, HD)
            o = (acc + a * oc[two].reshape(2 * CR, HD)) / total
            good = vc[...] > 0.5
            for h in range(2):
                v = jnp.where(good, o[h * CR : (h + 1) * CR], 0.0)
                ctx[k, c, :, (2 * u + h) * HD : (2 * u + h + 1) * HD] = v.astype(BF16)

    def ctx_copy(k, core):
        slot = ctx.at[k, core]
        return remote(slot, slot, c_send.at[k], c_recv.at[k], (bulk, tp_at(0, 0, oth)))

    def project(k, dy, dzh):
        n = lax.rem(zh + dzh, NZH) * NY + lax.rem(y + dy, NY)
        return jnp.dot(ctx[k, 0], wbuf[0, n], preferred_element_type=F32) + jnp.dot(
            ctx[k, 1], wbuf[1, n], preferred_element_type=F32
        )

    up, down = (bulk, tp_at(0, 1, c)), (bulk, tp_at(0, 3, c))
    toward = (up, down)

    def d2_copy(k, side):
        return remote(
            d2s.at[k, side], d2r.at[k, side], d2_send.at[k, side], d2_recv.at[k, side], toward[side]
        )

    def b_copy(k, side, dzh):
        return remote(
            bs.at[k, side, dzh],
            br.at[k, side, dzh],
            b_send.at[k, side, dzh],
            b_recv.at[k, side, dzh],
            toward[side],
        )

    def first_sends(k):
        ctx_copy(k, oth).wait_recv()
        for side in range(2):
            d2s[k, side] = project(k, 2, side).astype(BF16)
            d2_copy(k, side).start()
        for side in range(2):
            dzh = 1 - side
            bs[k, side, dzh] = project(k, 1 + 2 * side, dzh).astype(BF16)
            b_copy(k, side, dzh).start()

    def merged_sends(k):
        for side in range(2):
            mine = project(k, 1 + 2 * side, side)
            d2_copy(k, side).wait_recv()
            bs[k, side, side] = (mine + d2r[k, side].astype(F32)).astype(BF16)
            b_copy(k, side, side).start()

    def x_copy(k, dz, dzh):
        return remote(
            ds.at[k, dzh, pl.ds(dz * 32, 32), :],
            rx.at[k, dz, dzh],
            x_send.at[k, dz, dzh],
            x_recv.at[k, dz, dzh],
            (bulk_at(lax.rem(k + 1, NX), dz), tp_at(dzh, 0, c)),
        )

    def finish(k):
        def gather(i, carry):
            b = blk[k * 16 + i]
            n = nval[k * 16 + i]
            row = lax.broadcasted_iota(jnp.int32, (8, FE), 0)
            rc[pl.ds(pl.multiple_of(i * 8, 8), 8), :] = jnp.where(row < n, rf[b], 0.0)
            return carry

        lax.fori_loop(0, 16, gather, 0)
        for dzh in range(NZH):
            mine = project(k, 0, dzh)
            if dzh == 0:
                mine = mine + rc[...]
            for side in range(2):
                b_copy(k, side, dzh).wait_recv()
                mine = mine + br[k, side, dzh].astype(F32)
            ds[k, dzh] = mine.astype(BF16)
        for dzh in range(NZH):
            for dz in range(NZL):
                if dz or dzh:
                    x_copy(k, dz, dzh).start()
                else:

                    @pl.when(k < NK - 1)
                    def _():
                        x_copy(k, 0, 0).start()

    def w_from_sibling(n):
        return remote(
            w.at[:, pl.ds(0, FE)], wbuf.at[oth, n], w_send.at[n], w_recv.at[n], (bulk, tp_at(0, 0, oth))
        )

    def weights(n, carry):
        pltpu.make_async_copy(w.at[:, pl.ds(0, FE)], wbuf.at[c, n], w_loc.at[n]).wait()
        w_from_sibling(n).wait_recv()
        return carry

    def step(k, carry):
        @pl.when(k < NK)
        def _():
            attend(k)
            ctx_copy(k, c).start()

        @pl.when(k == 0)
        def _():
            lax.fori_loop(0, 8, weights, 0)

        @pl.when(k > 0)
        def _():
            merged_sends(k - 1)

        @pl.when(k < NK)
        def _():
            first_sends(k)

        @pl.when(k > 0)
        def _():
            finish(k - 1)

        return carry

    lax.fori_loop(0, NK + 1, step, 0)

    def collect(k, carry):
        dx = lax.rem(k + 1, NX)
        for dz in range(NZL):
            s = lax.rem(zl + NZL - dz, NZL) * NX + lax.rem(x + NX - dx, NX)
            x_copy(k, dz, 1).wait_recv()
            total = rx[k, dz, 1].astype(F32)
            if dz:
                x_copy(k, dz, 0).wait_recv()
            else:

                @pl.when(k < NK - 1)
                def _():
                    x_copy(k, 0, 0).wait_recv()

                @pl.when(k == NK - 1)
                def _():
                    rx[k, 0, 0] = ds[k, 0, 0:32, :]

            total = total + rx[k, dz, 0].astype(F32)
            out[pl.ds(pl.multiple_of(s * 32, 32), 32), :] = total.astype(BF16)
        return carry

    lax.fori_loop(0, NK, collect, 0)

    for j in range(1, 8):
        for copy in kv_copies(j):
            copy.wait_send()

    def left(n, carry):
        forward(n).wait_send()
        w_from_sibling(n).wait_send()
        return carry

    lax.fori_loop(0, 8, left, 0)

    def left_k(k, carry):
        ctx_copy(k, c).wait_send()
        for side in range(2):
            d2_copy(k, side).wait_send()
            for dzh in range(NZH):
                b_copy(k, side, dzh).wait_send()
        for dz in range(NZL):
            for dzh in range(NZH):
                if dz or dzh:
                    x_copy(k, dz, dzh).wait_send()
                else:

                    @pl.when(k < NK - 1)
                    def _():
                        x_copy(k, 0, 0).wait_send()

        return carry

    lax.fori_loop(0, NK, left_k, 0)


def local(queries, comp_keys, comp_values, prefix_keys, prefix_values, lengths, routing, residual, out_weight):
    smem = pl.BlockSpec(memory_space=pltpu.SMEM)
    anywhere = pl.BlockSpec(memory_space=pl.ANY)
    blk, nval = pl.pallas_call(
        tables_kernel,
        out_shape=[jax.ShapeDtypeStruct((64,), jnp.int32)] * 2,
        in_specs=[smem, smem],
        out_specs=[smem, smem],
        scratch_shapes=[pltpu.SMEM((16,), jnp.int32)],
        name="tables",
    )(lengths, routing)
    vmem = pltpu.VMEM
    dma = pltpu.SemaphoreType.DMA
    return pl.pallas_call(
        main_kernel,
        out_shape=jax.ShapeDtypeStruct((512, FE), BF16),
        in_specs=[smem, smem] + [anywhere] * 7,
        out_specs=pl.BlockSpec(memory_space=pltpu.VMEM),
        scratch_shapes=[
            vmem((8, 2, 384, HD), BF16),
            vmem((2, 8, 512, FE), BF16),
            vmem((1024, FE), BF16),
            vmem((1024, FE), BF16),
            vmem((128, 8, FE), F32),
            vmem((128, 8, FE), F32),
            vmem((128, 8, FE), F32),
            vmem((128, 8, FE), F32),
            vmem((128, 8, FE), F32),
            vmem((8, 2 * CR, 256), F32),
            vmem((LH, CR, HD), F32),
            vmem((LH, CR, HD), F32),
            vmem((LH, CR, HD), F32),
            vmem((LH, CR, HD), F32),
            vmem((CR, HD), F32),
            vmem((CR, FE), F32),
            vmem((NK, 2, CR, FE), BF16),
            vmem((NK, 2, CR, FE), BF16),
            vmem((NK, 2, CR, FE), BF16),
            vmem((NK, 2, 2, CR, FE), BF16),
            vmem((NK, 2, 2, CR, FE), BF16),
            vmem((NK, 2, CR, FE), BF16),
            vmem((NK, NZL, 2, 32, FE), BF16),
            dma, dma, dma((4,)), dma((8, 4)), dma((8, 4)), dma((8,)), dma((8,)),
            dma((8,)), dma((8,)), dma((8,)),
            dma((NK,)), dma((NK,)), dma((NK, 2)), dma((NK, 2)), dma((NK, 2, 2)), dma((NK, 2, 2)),
            dma((NK, NZL, 2)), dma((NK, NZL, 2)),
        ],
        compiler_params=pltpu.CompilerParams(
            collective_id=0, has_side_effects=True, vmem_limit_bytes=56 * 2**20
        ),
        name="attend_project_send",
    )(blk, nval, queries, comp_keys, comp_values, prefix_keys, prefix_values, residual, out_weight)


def solution(mesh):
    return jax.shard_map(
        local,
        mesh=mesh,
        in_specs=(
            P("bulk", "tp"),
            P(("bulk", "tp"), None),
            P(("bulk", "tp"), None),
            P("bulk", "tp", None),
            P("bulk", "tp", None),
            P("bulk", None),
            P("bulk", None),
            P("bulk", "tp"),
            P("tp", None),
        ),
        out_specs=P("bulk", "tp"),
        check_vma=False,
    )
```

```python
import math

import jax
import jax.numpy as jnp
from jax import lax
from jax.experimental import pallas as pl
from jax.experimental.pallas import tpu as pltpu
from jax.sharding import PartitionSpec as P

HD = 128
BLK = 8
NX, NY, NZL, NZH, NC = 4, 4, 4, 2, 2
NK = 4
DZ = NX * NZL // NK
CR = 512 // NK
CB = CR // BLK
LH = 4
FE = 512
SCALE = math.log2(math.e) / math.sqrt(HD)
F32, BF16 = jnp.float32, jnp.bfloat16
MESH = pl.DeviceIdType.MESH
NT = (((1,), (1,)), ((), ()))


def position():
    b, t = lax.axis_index("bulk"), lax.axis_index("tp")
    x, zl = lax.rem(b, NX), lax.div(b, NX)
    c, y, zh = lax.rem(t, NC), lax.rem(lax.div(t, NC), NY), lax.div(t, NC * NY)
    return x, zl, c, y, zh


def tables(lens, route, x, zl):
    sub = lax.broadcasted_iota(jnp.int32, (128, 128), 0)
    lane = lax.broadcasted_iota(jnp.int32, (128, 128), 1)
    size = jnp.zeros((128, 128), jnp.int32)
    for i in range(16):
        size = jnp.where((sub >> 3) == i, lens[0, i], size)
    first = (sub & 7) * BLK
    live = first < size
    one = jnp.where(live, 1, 0)
    rank = jnp.sum(jnp.where(sub < lane, one, 0), axis=0, keepdims=True)
    rank = jnp.sum(jnp.where(sub == lane, rank, 0), axis=1, keepdims=True)
    place = lax.broadcasted_iota(jnp.int32, (8, 128), 1)
    dest = jnp.full((8, 128), -1, jnp.int32)
    for j in range(64):
        dest = jnp.where(place == j, route[0, j], dest)
    dest = dest[0:1]
    down = jnp.sum(jnp.where(sub == lane, dest, 0), axis=1, keepdims=True)
    seen = jnp.sum(jnp.where((down == dest) & (sub < lane), 1, 0), axis=0, keepdims=True)
    k = ((dest & 3) - x + 2 * NX - 1) & 3
    dz = ((dest >> 2) - zl + NZL) & 3
    slot = (k * NZL + dz) * 4 + seen
    slot = jnp.sum(jnp.where((rank == lane) & live, slot, 0), axis=1, keepdims=True)
    here = (slot == lane) & live
    blk = jnp.sum(jnp.where(here, sub, 0), axis=0, keepdims=True)
    nval = jnp.sum(jnp.where(here, jnp.minimum(size - first, BLK), 0), axis=0, keepdims=True)
    return blk, nval


def main_kernel(
    lens, route, q, ck, cv, pk, pv, res, w, out0, out1,
    kv, wbuf, qv, rv, qf, rf, oown, mown, lown, scores, qc, oc, mc, lc, vc, rc,
    ctx, d2s, d2r, bs, br, ds, tab, order, met,
    t_sem, q_sem, r_sem, kv_loc, kv_send, kv_recv, fw_send, fw_recv, w_loc, w_send, w_recv,
    c_send, c_recv, d2_send, d2_recv, b_send, b_recv, x_send, x_recv,
):
    x, zl, c, y, zh = position()
    oth = 1 - c
    bulk = zl * NX + x

    def bulk_at(dx, dz):
        return lax.rem(zl + dz, NZL) * NX + lax.rem(x + dx, NX)

    def tp_at(dzh, dy, core):
        return (lax.rem(zh + dzh, NZH) * NY + lax.rem(y + dy, NY)) * NC + core

    def remote(src, dst, send, recv, where):
        return pltpu.make_async_remote_copy(
            src_ref=src, dst_ref=dst, send_sem=send, recv_sem=recv, device_id=where, device_id_type=MESH
        )

    q_copy = pltpu.make_async_copy(q, qv, q_sem)
    r_copy = pltpu.make_async_copy(res, rv, r_sem)
    q_copy.start()
    r_copy.start()

    barrier = pltpu.get_barrier_semaphore()
    peers = [(bulk, tp_at(dzh, dy, c)) for dzh in range(NZH) for dy in range(NY) if dzh or dy]
    peers += [(bulk, tp_at(0, 0, oth))]
    x_line = [(bulk_at(dx, 0), tp_at(0, 0, c)) for dx in (1, 3, 2)]
    z = zh * NZL + zl

    def z_at(dz):
        at = lax.rem(z + dz, NZH * NZL)
        return lax.rem(at, NZL) * NX + x, (lax.div(at, NZL) * NY + y) * NC + c

    z_near = [z_at(1), z_at(7)]
    peers += x_line[:2] + z_near
    for where in peers:
        pl.semaphore_signal(barrier, inc=1, device_id=where, device_id_type=MESH)
    pl.semaphore_wait(barrier, len(peers))

    parts = (
        (pk.at[0], 0, 128),
        (pv.at[0], 128, 128),
        (ck, 256, 64),
        (cv, 320, 64),
    )

    def kv_copies(j, chosen=range(4)):
        dzh, dy = j // NY, j % NY
        head = pl.multiple_of((lax.rem(zh + dzh, NZH) * NY + lax.rem(y + dy, NY)) * HD, HD)
        made = []
        for n in chosen:
            src, at, rows = parts[n]
            s = src.at[:, pl.ds(head, HD)]
            d = kv.at[j, c, pl.ds(at, rows), :]
            if j == 0:
                made.append(pltpu.make_async_copy(s, d, kv_loc.at[n]))
            else:
                made.append(remote(s, d, kv_send.at[j, n], kv_recv.at[j, n], (bulk, tp_at(dzh, dy, c))))
        return made

    for few in ((2, 3), (0, 1)):
        for j in (6, 5, 7, 4, 2, 1, 3, 0):
            for copy in kv_copies(j, few):
                copy.start()

    def w_copies(n):
        here = pltpu.make_async_copy(
            w.at[:, pl.ds(pl.multiple_of((2 * n + c) * FE, FE), FE)], wbuf.at[c, n], w_loc.at[n]
        )
        away = remote(
            w.at[:, pl.ds(pl.multiple_of((2 * n + oth) * FE, FE), FE)],
            wbuf.at[c, n],
            w_send.at[n],
            w_recv.at[n],
            (bulk, tp_at(0, 0, oth)),
        )
        return here, away

    for n in range(8):
        for copy in w_copies(n):
            copy.start()

    for n, known in enumerate((x_line[:2], z_near, z_near, x_line)):
        for where in known:
            pl.semaphore_signal(met.at[n], inc=1, device_id=where, device_id_type=MESH)
        pl.semaphore_wait(met.at[n], len(known))

    blk, nval = tables(lens, route, x, zl)
    tab[0:1, :] = blk
    tab[1:2, :] = nval
    t_copy = pltpu.make_async_copy(tab, order, t_sem)
    t_copy.start()
    q_copy.wait()
    r_copy.wait()
    t_copy.wait()

    def widen(i, carry):
        rows = pl.ds(pl.multiple_of(i * 64, 64), 64)
        at = pl.ds(i * 8, 8)
        qf[at] = qv[rows, :].astype(F32).reshape(8, 8, FE)
        rf[at] = rv[rows, :].astype(F32).reshape(8, 8, FE)
        return carry

    lax.fori_loop(0, 16, widen, 0)

    def own_part(j, core):
        dzh, dy = lax.div(j, NY), lax.rem(j, NY)
        i = (lax.rem(zh + NZH - dzh, NZH) * NY + lax.rem(y + NY - dy, NY)) * NC + core
        rows = pl.ds(pl.multiple_of(i * 64, 64), 64)
        at = pl.ds(i * 8, 8)
        qs = jnp.concatenate([qv[rows, h * HD : (h + 1) * HD] for h in range(LH)], axis=0)
        s = lax.dot_general(qs, kv[j, core, 256:320, :], NT, preferred_element_type=F32) * SCALE
        row = lax.broadcasted_iota(jnp.int32, s.shape, 0) & 63
        col = lax.broadcasted_iota(jnp.int32, s.shape, 1)
        s = jnp.where(col <= row, s, -1e30)
        m = jnp.max(s, axis=1, keepdims=True)
        e = jnp.exp2(s - m)
        total = jnp.sum(e, axis=1, keepdims=True)
        o = jnp.dot(e.astype(BF16), kv[j, core, 320:384, :], preferred_element_type=F32)
        m, total = jnp.broadcast_to(m, o.shape), jnp.broadcast_to(total, o.shape)
        for h in range(LH):
            cols = slice(h * HD, (h + 1) * HD)
            part = slice(h * 64, (h + 1) * 64)
            oown[at, :, cols] = o[part].reshape(8, 8, HD)
            mown[at, :, cols] = m[part].reshape(8, 8, HD)
            lown[at, :, cols] = total[part].reshape(8, 8, HD)

    pieces = (pl.ds(0, 256), pl.ds(256, 128))

    def forward(j, n):
        part = kv.at[j, c, pieces[n], :]
        return remote(part, part, fw_send.at[j, n], fw_recv.at[j, n], (bulk, tp_at(0, 0, oth)))

    def from_sibling(j, n):
        part = kv.at[j, oth, pieces[n], :]
        return remote(part, part, fw_send.at[j, n], fw_recv.at[j, n], (bulk, tp_at(0, 0, oth)))

    def arrived(j, n):
        for copy in kv_copies(j, (2 * n, 2 * n + 1)):
            if j == 0:
                copy.wait()
            else:
                copy.wait_recv()
        forward(j, n).start()

    near, late = (0, 1, 3, 2), (4, 5, 7, 6)
    for some in (near, late):
        for j in some:
            arrived(j, 1)
            own_part(j, c)
        for j in some:
            from_sibling(j, 1).wait_recv()
            own_part(j, oth)
    for j in near + late:
        arrived(j, 0)
    for j in near + late:
        from_sibling(j, 0).wait_recv()

    def attend(k):
        def gather(i, carry):
            b = order[0, k * CB + i]
            n = order[1, k * CB + i]
            at = pl.ds(pl.multiple_of(i * 8, 8), 8)
            qb, ob, mb, lb = qf[b], oown[b], mown[b], lown[b]
            for h in range(LH):
                cols = slice(h * HD, (h + 1) * HD)
                qc[h, at, :] = qb[:, cols]
                oc[h, at, :] = ob[:, cols]
                mc[h, at, :] = mb[:, cols]
                lc[h, at, :] = lb[:, cols]
            vc[at, :] = (lax.broadcasted_iota(jnp.int32, (8, HD), 0) < n).astype(F32)
            return carry

        lax.fori_loop(0, CB, gather, 0)

        rows = LH * CR
        qb = qc[...].reshape(rows, HD).astype(BF16)
        top = None
        for j in range(8):
            s = lax.dot_general(
                qb, kv[j, :, 0:128, :].reshape(256, HD), NT, preferred_element_type=F32
            )
            scores[j] = s
            both = jnp.maximum(s[:, :HD], s[:, HD:])
            top = both if top is None else jnp.maximum(top, both)
        m_own = mc[...].reshape(rows, HD)
        m = jnp.maximum(jnp.max(top, axis=1, keepdims=True) * SCALE, m_own)
        wide = jnp.concatenate([m, m], axis=1)
        acc = jnp.zeros((rows, HD), F32)
        sums = jnp.zeros((rows, HD), F32)
        for j in range(8):
            e = jnp.exp2(scores[j] * SCALE - wide)
            sums = sums + (e[:, :HD] + e[:, HD:])
            acc = acc + jnp.dot(
                e.astype(BF16), kv[j, :, 128:256, :].reshape(256, HD), preferred_element_type=F32
            )
        a = jnp.exp2(m_own - m)
        total = jnp.sum(sums, axis=1, keepdims=True) + a * lc[...].reshape(rows, HD)
        o = (acc + a * oc[...].reshape(rows, HD)) / total
        good = vc[...] > 0.5
        for h in range(LH):
            v = jnp.where(good, o[h * CR : (h + 1) * CR], 0.0)
            ctx[k, c, :, h * HD : (h + 1) * HD] = v.astype(BF16)

    def ctx_copy(k, core):
        slot = ctx.at[k, core]
        return remote(slot, slot, c_send.at[k], c_recv.at[k], (bulk, tp_at(0, 0, oth)))

    def project(k, dy, dzh):
        n = lax.rem(zh + dzh, NZH) * NY + lax.rem(y + dy, NY)
        return jnp.dot(ctx[k, 0], wbuf[0, n], preferred_element_type=F32) + jnp.dot(
            ctx[k, 1], wbuf[1, n], preferred_element_type=F32
        )

    up, down = (bulk, tp_at(0, 1, c)), (bulk, tp_at(0, 3, c))
    toward = (up, down)

    def d2_copy(k, side):
        return remote(
            d2s.at[k, side], d2r.at[k, side], d2_send.at[k, side], d2_recv.at[k, side], toward[side]
        )

    def b_copy(k, side, dzh):
        return remote(
            bs.at[k, side, dzh],
            br.at[k, side, dzh],
            b_send.at[k, side, dzh],
            b_recv.at[k, side, dzh],
            toward[side],
        )

    def first_sends(k):
        ctx_copy(k, oth).wait_recv()
        for side in range(2):
            d2s[k, side] = project(k, 2, side).astype(BF16)
            d2_copy(k, side).start()
        for side in range(2):
            dzh = 1 - side
            bs[k, side, dzh] = project(k, 1 + 2 * side, dzh).astype(BF16)
            b_copy(k, side, dzh).start()

    def merged_sends(k):
        for side in range(2):
            mine = project(k, 1 + 2 * side, side)
            d2_copy(k, side).wait_recv()
            bs[k, side, side] = (mine + d2r[k, side].astype(F32)).astype(BF16)
            b_copy(k, side, side).start()

    mine32 = pl.ds(pl.multiple_of(bulk * 32, 32), 32)
    outs = (out0, out1)

    def x_copy(k, n, dzh):
        return remote(
            ds.at[k, dzh, pl.ds(n * 32, 32), :],
            outs[dzh].at[mine32, :],
            x_send.at[k, n, dzh],
            x_recv.at[k, n, dzh],
            (bulk_at(lax.rem(lax.div(k, NK // NX) + 1, NX), lax.rem(k, NK // NX) * DZ + n), tp_at(dzh, 0, c)),
        )

    def stay():
        return pltpu.make_async_copy(ds.at[NK - NK // NX, 0, 0:32, :], out0.at[mine32, :], q_sem)

    def x_each(k, do):
        for dzh in range(NZH):
            for n in range(DZ):
                if n or dzh:
                    do(x_copy(k, n, dzh))
                else:

                    @pl.when(k != NK - NK // NX)
                    def _():
                        do(x_copy(k, 0, 0))

    def finish(k):
        def gather(i, carry):
            b = order[0, k * CB + i]
            n = order[1, k * CB + i]
            row = lax.broadcasted_iota(jnp.int32, (8, FE), 0)
            rc[pl.ds(pl.multiple_of(i * 8, 8), 8), :] = jnp.where(row < n, rf[b], 0.0)
            return carry

        lax.fori_loop(0, CB, gather, 0)
        for dzh in range(NZH):
            mine = project(k, 0, dzh)
            if dzh == 0:
                mine = mine + rc[...]
            for side in range(2):
                b_copy(k, side, dzh).wait_recv()
                mine = mine + br[k, side, dzh].astype(F32)
            ds[k, dzh] = mine.astype(BF16)
        x_each(k, lambda copy: copy.start())

        @pl.when(k == NK - NK // NX)
        def _():
            stay().start()

    def w_from_sibling(n):
        return remote(
            w.at[:, pl.ds(0, FE)], wbuf.at[oth, n], w_send.at[n], w_recv.at[n], (bulk, tp_at(0, 0, oth))
        )

    def weights(n, carry):
        pltpu.make_async_copy(w.at[:, pl.ds(0, FE)], wbuf.at[c, n], w_loc.at[n]).wait()
        w_from_sibling(n).wait_recv()
        return carry

    def step(k, carry):
        @pl.when(k < NK)
        def _():
            attend(k)
            ctx_copy(k, c).start()

        @pl.when(k == 0)
        def _():
            lax.fori_loop(0, 8, weights, 0)

        @pl.when(k > 0)
        def _():
            merged_sends(k - 1)

        @pl.when(k < NK)
        def _():
            first_sends(k)

        @pl.when(k > 0)
        def _():
            finish(k - 1)

        return carry

    lax.fori_loop(0, NK + 1, step, 0)

    def collect(k, carry):
        x_each(k, lambda copy: copy.wait_recv())
        return carry

    lax.fori_loop(0, NK, collect, 0)
    stay().wait()

    for j in range(1, 8):
        for copy in kv_copies(j):
            copy.wait_send()

    def left(n, carry):
        for part in range(2):
            forward(n, part).wait_send()
        w_from_sibling(n).wait_send()
        return carry

    lax.fori_loop(0, 8, left, 0)

    def left_k(k, carry):
        ctx_copy(k, c).wait_send()
        for side in range(2):
            d2_copy(k, side).wait_send()
            for dzh in range(NZH):
                b_copy(k, side, dzh).wait_send()
        x_each(k, lambda copy: copy.wait_send())
        return carry

    lax.fori_loop(0, NK, left_k, 0)


def local(queries, comp_keys, comp_values, prefix_keys, prefix_values, lengths, routing, residual, out_weight):
    smem = pl.BlockSpec(memory_space=pltpu.SMEM)
    anywhere = pl.BlockSpec(memory_space=pl.ANY)
    vmem = pltpu.VMEM
    dma = pltpu.SemaphoreType.DMA
    near, far = pl.pallas_call(
        main_kernel,
        out_shape=[jax.ShapeDtypeStruct((512, FE), BF16)] * 2,
        in_specs=[smem, smem] + [anywhere] * 7,
        out_specs=[anywhere] * 2,
        scratch_shapes=[
            vmem((8, 2, 384, HD), BF16),
            vmem((2, 8, 512, FE), BF16),
            vmem((1024, FE), BF16),
            vmem((1024, FE), BF16),
            vmem((128, 8, FE), F32),
            vmem((128, 8, FE), F32),
            vmem((128, 8, FE), F32),
            vmem((128, 8, FE), F32),
            vmem((128, 8, FE), F32),
            vmem((8, LH * CR, 256), F32),
            vmem((LH, CR, HD), F32),
            vmem((LH, CR, HD), F32),
            vmem((LH, CR, HD), F32),
            vmem((LH, CR, HD), F32),
            vmem((CR, HD), F32),
            vmem((CR, FE), F32),
            vmem((NK, 2, CR, FE), BF16),
            vmem((NK, 2, CR, FE), BF16),
            vmem((NK, 2, CR, FE), BF16),
            vmem((NK, 2, 2, CR, FE), BF16),
            vmem((NK, 2, 2, CR, FE), BF16),
            vmem((NK, 2, CR, FE), BF16),
            vmem((8, 128), jnp.int32),
            pltpu.SMEM((8, 128), jnp.int32),
            pltpu.SemaphoreType.REGULAR((4,)),
            dma,
            dma, dma, dma((4,)), dma((8, 4)), dma((8, 4)), dma((8, 2)), dma((8, 2)),
            dma((8,)), dma((8,)), dma((8,)),
            dma((NK,)), dma((NK,)), dma((NK, 2)), dma((NK, 2)), dma((NK, 2, 2)), dma((NK, 2, 2)),
            dma((NK, DZ, 2)), dma((NK, DZ, 2)),
        ],
        compiler_params=pltpu.CompilerParams(
            collective_id=0, has_side_effects=True, vmem_limit_bytes=56 * 2**20
        ),
        name="attend_project_send",
    )(lengths, routing, queries, comp_keys, comp_values, prefix_keys, prefix_values, residual, out_weight)
    return (near.astype(F32) + far.astype(F32)).astype(BF16)


def solution(mesh):
    return jax.shard_map(
        local,
        mesh=mesh,
        in_specs=(
            P("bulk", "tp"),
            P(("bulk", "tp"), None),
            P(("bulk", "tp"), None),
            P("bulk", "tp", None),
            P("bulk", "tp", None),
            P("bulk", None),
            P("bulk", None),
            P("bulk", "tp"),
            P("tp", None),
        ),
        out_specs=P("bulk", "tp"),
        check_vma=False,
    )
```

```python
import math

import jax
import jax.numpy as jnp
from jax import lax
from jax.experimental import pallas as pl
from jax.experimental.pallas import tpu as pltpu
from jax.sharding import PartitionSpec as P

HD = 128
BLK = 8
NX, NY, NZL, NZH, NC = 4, 4, 4, 2, 2
NK = 4
DZ = NX * NZL // NK
CR = 512 // NK
CB = CR // BLK
LH = 4
FE = 512
SCALE = math.log2(math.e) / math.sqrt(HD)
F32, BF16 = jnp.float32, jnp.bfloat16
MESH = pl.DeviceIdType.MESH
NT = (((1,), (1,)), ((), ()))


def position():
    b, t = lax.axis_index("bulk"), lax.axis_index("tp")
    x, zl = lax.rem(b, NX), lax.div(b, NX)
    c, y, zh = lax.rem(t, NC), lax.rem(lax.div(t, NC), NY), lax.div(t, NC * NY)
    return x, zl, c, y, zh


def tables(lens, route, x, zl):
    sub = lax.broadcasted_iota(jnp.int32, (128, 128), 0)
    lane = lax.broadcasted_iota(jnp.int32, (128, 128), 1)
    size = jnp.zeros((128, 128), jnp.int32)
    for i in range(16):
        size = jnp.where((sub >> 3) == i, lens[0, i], size)
    first = (sub & 7) * BLK
    live = first < size
    one = jnp.where(live, 1, 0)
    rank = jnp.sum(jnp.where(sub < lane, one, 0), axis=0, keepdims=True)
    rank = jnp.sum(jnp.where(sub == lane, rank, 0), axis=1, keepdims=True)
    place = lax.broadcasted_iota(jnp.int32, (8, 128), 1)
    dest = jnp.full((8, 128), -1, jnp.int32)
    for j in range(64):
        dest = jnp.where(place == j, route[0, j], dest)
    dest = dest[0:1]
    down = jnp.sum(jnp.where(sub == lane, dest, 0), axis=1, keepdims=True)
    seen = jnp.sum(jnp.where((down == dest) & (sub < lane), 1, 0), axis=0, keepdims=True)
    k = ((dest & 3) - x + 2 * NX - 1) & 3
    dz = ((dest >> 2) - zl + NZL) & 3
    slot = (k * NZL + dz) * 4 + seen
    slot = jnp.sum(jnp.where((rank == lane) & live, slot, 0), axis=1, keepdims=True)
    here = (slot == lane) & live
    blk = jnp.sum(jnp.where(here, sub, 0), axis=0, keepdims=True)
    nval = jnp.sum(jnp.where(here, jnp.minimum(size - first, BLK), 0), axis=0, keepdims=True)
    return blk, nval


def main_kernel(
    lens, route, q, ck, cv, pk, pv, res, w, out,
    kv, wbuf, qv, rv, qf, rf, oown, mown, lown, scores, qc, oc, mc, lc, vc, rc,
    ctx, d2s, d2r, bs, br, ds, tab, order, met,
    t_sem, q_sem, r_sem, kv_loc, kv_send, kv_recv, fw_send, fw_recv, w_loc, w_send, w_recv,
    c_send, c_recv, d2_send, d2_recv, b_send, b_recv, x_send, x_recv,
):
    x, zl, c, y, zh = position()
    oth = 1 - c
    bulk = zl * NX + x

    def bulk_at(dx, dz):
        return lax.rem(zl + dz, NZL) * NX + lax.rem(x + dx, NX)

    def tp_at(dzh, dy, core):
        return (lax.rem(zh + dzh, NZH) * NY + lax.rem(y + dy, NY)) * NC + core

    def remote(src, dst, send, recv, where):
        return pltpu.make_async_remote_copy(
            src_ref=src, dst_ref=dst, send_sem=send, recv_sem=recv, device_id=where, device_id_type=MESH
        )

    q_copy = pltpu.make_async_copy(q, qv, q_sem)
    r_copy = pltpu.make_async_copy(res, rv, r_sem)
    q_copy.start()
    r_copy.start()

    barrier = pltpu.get_barrier_semaphore()
    peers = [(bulk, tp_at(dzh, dy, c)) for dzh in range(NZH) for dy in range(NY) if dzh or dy]
    peers += [(bulk, tp_at(0, 0, oth))]
    x_line = [(bulk_at(dx, 0), tp_at(0, 0, c)) for dx in (1, 3, 2)]
    z = zh * NZL + zl

    def z_at(dz):
        at = lax.rem(z + dz, NZH * NZL)
        return lax.rem(at, NZL) * NX + x, (lax.div(at, NZL) * NY + y) * NC + c

    z_near = [z_at(1), z_at(7)]
    peers += x_line[:2] + z_near
    for where in peers:
        pl.semaphore_signal(barrier, inc=1, device_id=where, device_id_type=MESH)
    pl.semaphore_wait(barrier, len(peers))

    parts = (
        (pk.at[0], 0, 128),
        (pv.at[0], 128, 128),
        (ck, 256, 64),
        (cv, 320, 64),
    )

    def kv_copies(j, chosen=range(4)):
        dzh, dy = j // NY, j % NY
        head = pl.multiple_of((lax.rem(zh + dzh, NZH) * NY + lax.rem(y + dy, NY)) * HD, HD)
        made = []
        for n in chosen:
            src, at, rows = parts[n]
            s = src.at[:, pl.ds(head, HD)]
            d = kv.at[j, c, pl.ds(at, rows), :]
            if j == 0:
                made.append(pltpu.make_async_copy(s, d, kv_loc.at[n]))
            else:
                made.append(remote(s, d, kv_send.at[j, n], kv_recv.at[j, n], (bulk, tp_at(dzh, dy, c))))
        return made

    for few in ((2, 3), (0,), (1,)):
        for j in (6, 5, 7, 4, 2, 1, 3, 0):
            for copy in kv_copies(j, few):
                copy.start()

    def w_copies(n):
        here = pltpu.make_async_copy(
            w.at[:, pl.ds(pl.multiple_of((2 * n + c) * FE, FE), FE)], wbuf.at[c, n], w_loc.at[n]
        )
        away = remote(
            w.at[:, pl.ds(pl.multiple_of((2 * n + oth) * FE, FE), FE)],
            wbuf.at[c, n],
            w_send.at[n],
            w_recv.at[n],
            (bulk, tp_at(0, 0, oth)),
        )
        return here, away

    for n in range(8):
        for copy in w_copies(n):
            copy.start()

    for n, known in enumerate((x_line[:2], z_near, z_near, x_line)):
        for where in known:
            pl.semaphore_signal(met.at[n], inc=1, device_id=where, device_id_type=MESH)
        pl.semaphore_wait(met.at[n], len(known))

    blk, nval = tables(lens, route, x, zl)
    tab[0:1, :] = blk
    tab[1:2, :] = nval
    t_copy = pltpu.make_async_copy(tab, order, t_sem)
    t_copy.start()
    q_copy.wait()
    r_copy.wait()
    t_copy.wait()

    def widen(i, carry):
        rows = pl.ds(pl.multiple_of(i * 64, 64), 64)
        at = pl.ds(i * 8, 8)
        qf[at] = qv[rows, :].astype(F32).reshape(8, 8, FE)
        rf[at] = rv[rows, :].astype(F32).reshape(8, 8, FE)
        return carry

    lax.fori_loop(0, 16, widen, 0)

    def own_part(j, core):
        dzh, dy = lax.div(j, NY), lax.rem(j, NY)
        i = (lax.rem(zh + NZH - dzh, NZH) * NY + lax.rem(y + NY - dy, NY)) * NC + core
        rows = pl.ds(pl.multiple_of(i * 64, 64), 64)
        at = pl.ds(i * 8, 8)
        qs = jnp.concatenate([qv[rows, h * HD : (h + 1) * HD] for h in range(LH)], axis=0)
        s = lax.dot_general(qs, kv[j, core, 256:320, :], NT, preferred_element_type=F32) * SCALE
        row = lax.broadcasted_iota(jnp.int32, s.shape, 0) & 63
        col = lax.broadcasted_iota(jnp.int32, s.shape, 1)
        s = jnp.where(col <= row, s, -1e30)
        m = jnp.max(s, axis=1, keepdims=True)
        e = jnp.exp2(s - m)
        total = jnp.sum(e, axis=1, keepdims=True)
        o = jnp.dot(e.astype(BF16), kv[j, core, 320:384, :], preferred_element_type=F32)
        m, total = jnp.broadcast_to(m, o.shape), jnp.broadcast_to(total, o.shape)
        for h in range(LH):
            cols = slice(h * HD, (h + 1) * HD)
            part = slice(h * 64, (h + 1) * 64)
            oown[at, :, cols] = o[part].reshape(8, 8, HD)
            mown[at, :, cols] = m[part].reshape(8, 8, HD)
            lown[at, :, cols] = total[part].reshape(8, 8, HD)

    pieces = ((256, 128, (2, 3)), (0, 128, (0,)), (128, 128, (1,)))

    def forward(j, n):
        part = kv.at[j, c, pl.ds(*pieces[n][:2]), :]
        return remote(part, part, fw_send.at[j, n], fw_recv.at[j, n], (bulk, tp_at(0, 0, oth)))

    def from_sibling(j, n):
        part = kv.at[j, oth, pl.ds(*pieces[n][:2]), :]
        return remote(part, part, fw_send.at[j, n], fw_recv.at[j, n], (bulk, tp_at(0, 0, oth)))

    def arrived(j, n):
        for copy in kv_copies(j, pieces[n][2]):
            if j == 0:
                copy.wait()
            else:
                copy.wait_recv()
        forward(j, n).start()

    near, late = (0, 1, 3, 2), (4, 5, 7, 6)
    for some in (near, late):
        for j in some:
            arrived(j, 0)
            own_part(j, c)
        for j in some:
            from_sibling(j, 0).wait_recv()
            own_part(j, oth)

    def all_here(n):
        for j in near + late:
            arrived(j, n)
        for j in near + late:
            from_sibling(j, n).wait_recv()

    def attend(k, first=False):
        def gather(i, carry):
            b = order[0, k * CB + i]
            n = order[1, k * CB + i]
            at = pl.ds(pl.multiple_of(i * 8, 8), 8)
            qb, ob, mb, lb = qf[b], oown[b], mown[b], lown[b]
            for h in range(LH):
                cols = slice(h * HD, (h + 1) * HD)
                qc[h, at, :] = qb[:, cols]
                oc[h, at, :] = ob[:, cols]
                mc[h, at, :] = mb[:, cols]
                lc[h, at, :] = lb[:, cols]
            vc[at, :] = (lax.broadcasted_iota(jnp.int32, (8, HD), 0) < n).astype(F32)
            return carry

        lax.fori_loop(0, CB, gather, 0)

        if first:
            all_here(1)
        rows = LH * CR
        qb = qc[...].reshape(rows, HD).astype(BF16)
        top = None
        for j in range(8):
            s = lax.dot_general(
                qb, kv[j, :, 0:128, :].reshape(256, HD), NT, preferred_element_type=F32
            )
            scores[j] = s
            both = jnp.maximum(s[:, :HD], s[:, HD:])
            top = both if top is None else jnp.maximum(top, both)
        m_own = mc[...].reshape(rows, HD)
        m = jnp.maximum(jnp.max(top, axis=1, keepdims=True) * SCALE, m_own)
        wide = jnp.concatenate([m, m], axis=1)
        if first:
            all_here(2)
        acc = jnp.zeros((rows, HD), F32)
        sums = jnp.zeros((rows, HD), F32)
        for j in range(8):
            e = jnp.exp2(scores[j] * SCALE - wide)
            sums = sums + (e[:, :HD] + e[:, HD:])
            acc = acc + jnp.dot(
                e.astype(BF16), kv[j, :, 128:256, :].reshape(256, HD), preferred_element_type=F32
            )
        a = jnp.exp2(m_own - m)
        total = jnp.sum(sums, axis=1, keepdims=True) + a * lc[...].reshape(rows, HD)
        o = (acc + a * oc[...].reshape(rows, HD)) / total
        good = vc[...] > 0.5
        for h in range(LH):
            v = jnp.where(good, o[h * CR : (h + 1) * CR], 0.0)
            ctx[k, c, :, h * HD : (h + 1) * HD] = v.astype(BF16)

    def ctx_copy(k, core):
        slot = ctx.at[k, core]
        return remote(slot, slot, c_send.at[k], c_recv.at[k], (bulk, tp_at(0, 0, oth)))

    def project(k, dy, dzh):
        n = lax.rem(zh + dzh, NZH) * NY + lax.rem(y + dy, NY)
        return jnp.dot(ctx[k, 0], wbuf[0, n], preferred_element_type=F32) + jnp.dot(
            ctx[k, 1], wbuf[1, n], preferred_element_type=F32
        )

    up, down = (bulk, tp_at(0, 1, c)), (bulk, tp_at(0, 3, c))
    toward = (up, down)

    def d2_copy(k, side):
        return remote(
            d2s.at[k, side], d2r.at[k, side], d2_send.at[k, side], d2_recv.at[k, side], toward[side]
        )

    def b_copy(k, side, dzh):
        return remote(
            bs.at[k, side, dzh],
            br.at[k, side, dzh],
            b_send.at[k, side, dzh],
            b_recv.at[k, side, dzh],
            toward[side],
        )

    def first_sends(k):
        ctx_copy(k, oth).wait_recv()
        for side in range(2):
            d2s[k, side] = project(k, 2, side).astype(BF16)
            d2_copy(k, side).start()
        for side in range(2):
            dzh = 1 - side
            bs[k, side, dzh] = project(k, 1 + 2 * side, dzh).astype(BF16)
            b_copy(k, side, dzh).start()

    def merged_sends(k):
        for side in range(2):
            mine = project(k, 1 + 2 * side, side)
            d2_copy(k, side).wait_recv()
            bs[k, side, side] = (mine + d2r[k, side].astype(F32)).astype(BF16)
            b_copy(k, side, side).start()

    mine32 = pl.ds(pl.multiple_of(bulk * 32, 32), 32)

    def x_copy(k, n, dzh):
        return remote(
            ds.at[k, dzh, pl.ds(n * 32, 32), :],
            out.at[dzh, mine32, :],
            x_send.at[k, n, dzh],
            x_recv.at[k, n, dzh],
            (bulk_at(lax.rem(lax.div(k, NK // NX) + 1, NX), lax.rem(k, NK // NX) * DZ + n), tp_at(dzh, 0, c)),
        )

    def stay():
        return pltpu.make_async_copy(ds.at[NK - NK // NX, 0, 0:32, :], out.at[0, mine32, :], q_sem)

    def x_half(k, dzh, do):
        for n in range(DZ):
            if n or dzh:
                do(x_copy(k, n, dzh))
            else:

                @pl.when(k != NK - NK // NX)
                def _():
                    do(x_copy(k, 0, 0))

    def x_each(k, do):
        for dzh in range(NZH):
            x_half(k, dzh, do)

    def finish(k):
        def gather(i, carry):
            b = order[0, k * CB + i]
            n = order[1, k * CB + i]
            row = lax.broadcasted_iota(jnp.int32, (8, FE), 0)
            rc[pl.ds(pl.multiple_of(i * 8, 8), 8), :] = jnp.where(row < n, rf[b], 0.0)
            return carry

        lax.fori_loop(0, CB, gather, 0)
        for dzh in (1, 0):
            mine = project(k, 0, dzh)
            if dzh == 0:
                mine = mine + rc[...]
            for side in (1 - dzh, dzh):
                b_copy(k, side, dzh).wait_recv()
                mine = mine + br[k, side, dzh].astype(F32)
            ds[k, dzh] = mine.astype(BF16)
            x_half(k, dzh, lambda copy: copy.start())

        @pl.when(k == NK - NK // NX)
        def _():
            stay().start()

    def w_from_sibling(n):
        return remote(
            w.at[:, pl.ds(0, FE)], wbuf.at[oth, n], w_send.at[n], w_recv.at[n], (bulk, tp_at(0, 0, oth))
        )

    def weights(n, carry):
        pltpu.make_async_copy(w.at[:, pl.ds(0, FE)], wbuf.at[c, n], w_loc.at[n]).wait()
        w_from_sibling(n).wait_recv()
        return carry

    attend(0, first=True)
    ctx_copy(0, c).start()
    lax.fori_loop(0, 8, weights, 0)

    def step(k, carry):
        @pl.when(k > 0)
        def _():
            merged_sends(k - 1)

        @pl.when(k < NK)
        def _():
            first_sends(k)

        @pl.when(k < NK - 1)
        def _():
            attend(k + 1)
            ctx_copy(k + 1, c).start()

        @pl.when(k > 0)
        def _():
            finish(k - 1)

        return carry

    lax.fori_loop(0, NK + 1, step, 0)

    def collect(k, carry):
        x_each(k, lambda copy: copy.wait_recv())
        return carry

    lax.fori_loop(0, NK, collect, 0)
    stay().wait()

    for j in range(1, 8):
        for copy in kv_copies(j):
            copy.wait_send()

    def left(n, carry):
        for part in range(3):
            forward(n, part).wait_send()
        w_from_sibling(n).wait_send()
        return carry

    lax.fori_loop(0, 8, left, 0)

    def left_k(k, carry):
        ctx_copy(k, c).wait_send()
        for side in range(2):
            d2_copy(k, side).wait_send()
            for dzh in range(NZH):
                b_copy(k, side, dzh).wait_send()
        x_each(k, lambda copy: copy.wait_send())
        return carry

    lax.fori_loop(0, NK, left_k, 0)


def local(queries, comp_keys, comp_values, prefix_keys, prefix_values, lengths, routing, residual, out_weight):
    smem = pl.BlockSpec(memory_space=pltpu.SMEM)
    anywhere = pl.BlockSpec(memory_space=pl.ANY)
    vmem = pltpu.VMEM
    dma = pltpu.SemaphoreType.DMA
    both = pl.pallas_call(
        main_kernel,
        out_shape=pltpu.VMEM((NZH, 512, FE), BF16),
        in_specs=[smem, smem] + [anywhere] * 7,
        out_specs=pl.BlockSpec(memory_space=pltpu.VMEM),
        scratch_shapes=[
            vmem((8, 2, 384, HD), BF16),
            vmem((2, 8, 512, FE), BF16),
            vmem((1024, FE), BF16),
            vmem((1024, FE), BF16),
            vmem((128, 8, FE), F32),
            vmem((128, 8, FE), F32),
            vmem((128, 8, FE), F32),
            vmem((128, 8, FE), F32),
            vmem((128, 8, FE), F32),
            vmem((8, LH * CR, 256), F32),
            vmem((LH, CR, HD), F32),
            vmem((LH, CR, HD), F32),
            vmem((LH, CR, HD), F32),
            vmem((LH, CR, HD), F32),
            vmem((CR, HD), F32),
            vmem((CR, FE), F32),
            vmem((NK, 2, CR, FE), BF16),
            vmem((NK, 2, CR, FE), BF16),
            vmem((NK, 2, CR, FE), BF16),
            vmem((NK, 2, 2, CR, FE), BF16),
            vmem((NK, 2, 2, CR, FE), BF16),
            vmem((NK, 2, CR, FE), BF16),
            vmem((8, 128), jnp.int32),
            pltpu.SMEM((8, 128), jnp.int32),
            pltpu.SemaphoreType.REGULAR((4,)),
            dma,
            dma, dma, dma((4,)), dma((8, 4)), dma((8, 4)), dma((8, 3)), dma((8, 3)),
            dma((8,)), dma((8,)), dma((8,)),
            dma((NK,)), dma((NK,)), dma((NK, 2)), dma((NK, 2)), dma((NK, 2, 2)), dma((NK, 2, 2)),
            dma((NK, DZ, 2)), dma((NK, DZ, 2)),
        ],
        compiler_params=pltpu.CompilerParams(
            collective_id=0, has_side_effects=True, vmem_limit_bytes=56 * 2**20
        ),
        name="attend_project_send",
    )(lengths, routing, queries, comp_keys, comp_values, prefix_keys, prefix_values, residual, out_weight)
    return (both[0].astype(F32) + both[1].astype(F32)).astype(BF16)


def solution(mesh):
    return jax.shard_map(
        local,
        mesh=mesh,
        in_specs=(
            P("bulk", "tp"),
            P(("bulk", "tp"), None),
            P(("bulk", "tp"), None),
            P("bulk", "tp", None),
            P("bulk", "tp", None),
            P("bulk", None),
            P("bulk", None),
            P("bulk", "tp"),
            P("tp", None),
        ),
        out_specs=P("bulk", "tp"),
        check_vma=False,
    )
```

```python
import math

import jax
import jax.numpy as jnp
from jax import lax
from jax.experimental import pallas as pl
from jax.experimental.pallas import tpu as pltpu
from jax.sharding import PartitionSpec as P

HD = 128
BLK = 8
NX, NY, NZL, NZH, NC = 4, 4, 4, 2, 2
SEND = 32
CHUNKS = (96, 160, 160, 96)
NK = len(CHUNKS)
STARTS = tuple(sum(CHUNKS[:k]) for k in range(NK))
CR = max(CHUNKS)
ND = NX * NZL
STAYS = ND - NZL
LH = 4
FE = 512
SCALE = math.log2(math.e) / math.sqrt(HD)
F32, BF16 = jnp.float32, jnp.bfloat16
MESH = pl.DeviceIdType.MESH
NT = (((1,), (1,)), ((), ()))


def position():
    b, t = lax.axis_index("bulk"), lax.axis_index("tp")
    x, zl = lax.rem(b, NX), lax.div(b, NX)
    c, y, zh = lax.rem(t, NC), lax.rem(lax.div(t, NC), NY), lax.div(t, NC * NY)
    return x, zl, c, y, zh


def tables(lens, route, x, zl):
    sub = lax.broadcasted_iota(jnp.int32, (128, 128), 0)
    lane = lax.broadcasted_iota(jnp.int32, (128, 128), 1)
    size = jnp.zeros((128, 128), jnp.int32)
    for i in range(16):
        size = jnp.where((sub >> 3) == i, lens[0, i], size)
    first = (sub & 7) * BLK
    live = first < size
    one = jnp.where(live, 1, 0)
    rank = jnp.sum(jnp.where(sub < lane, one, 0), axis=0, keepdims=True)
    rank = jnp.sum(jnp.where(sub == lane, rank, 0), axis=1, keepdims=True)
    place = lax.broadcasted_iota(jnp.int32, (8, 128), 1)
    dest = jnp.full((8, 128), -1, jnp.int32)
    for j in range(64):
        dest = jnp.where(place == j, route[0, j], dest)
    dest = dest[0:1]
    down = jnp.sum(jnp.where(sub == lane, dest, 0), axis=1, keepdims=True)
    seen = jnp.sum(jnp.where((down == dest) & (sub < lane), 1, 0), axis=0, keepdims=True)
    k = ((dest & 3) - x + 2 * NX - 1) & 3
    dz = ((dest >> 2) - zl + NZL) & 3
    slot = (k * NZL + dz) * 4 + seen
    slot = jnp.sum(jnp.where((rank == lane) & live, slot, 0), axis=1, keepdims=True)
    here = (slot == lane) & live
    blk = jnp.sum(jnp.where(here, sub, 0), axis=0, keepdims=True)
    nval = jnp.sum(jnp.where(here, jnp.minimum(size - first, BLK), 0), axis=0, keepdims=True)
    return blk, nval


def main_kernel(
    lens, route, q, ck, cv, pk, pv, res, w, out,
    kv, wbuf, qv, rv, qf, rf, oown, mown, lown, scores, qc, oc, mc, lc, vc, rc,
    ctx, d2s, d2r, bs, br, ds, tab, order, met,
    t_sem, q_sem, r_sem, kv_loc, kv_send, kv_recv, fw_send, fw_recv, w_loc, w_send, w_recv,
    c_send, c_recv, d2_send, d2_recv, b_send, b_recv, x_send, x_recv,
):
    x, zl, c, y, zh = position()
    oth = 1 - c
    bulk = zl * NX + x

    def bulk_at(dx, dz):
        return lax.rem(zl + dz, NZL) * NX + lax.rem(x + dx, NX)

    def tp_at(dzh, dy, core):
        return (lax.rem(zh + dzh, NZH) * NY + lax.rem(y + dy, NY)) * NC + core

    def remote(src, dst, send, recv, where):
        return pltpu.make_async_remote_copy(
            src_ref=src, dst_ref=dst, send_sem=send, recv_sem=recv, device_id=where, device_id_type=MESH
        )

    q_copy = pltpu.make_async_copy(q, qv, q_sem)
    r_copy = pltpu.make_async_copy(res, rv, r_sem)
    q_copy.start()
    r_copy.start()

    barrier = pltpu.get_barrier_semaphore()
    peers = [(bulk, tp_at(dzh, dy, c)) for dzh in range(NZH) for dy in range(NY) if dzh or dy]
    peers += [(bulk, tp_at(0, 0, oth))]
    x_line = [(bulk_at(dx, 0), tp_at(0, 0, c)) for dx in (1, 3, 2)]
    z = zh * NZL + zl

    def z_at(dz):
        at = lax.rem(z + dz, NZH * NZL)
        return lax.rem(at, NZL) * NX + x, (lax.div(at, NZL) * NY + y) * NC + c

    z_near = [z_at(1), z_at(7)]
    peers += [x_line[1], z_near[1]]
    for where in peers:
        pl.semaphore_signal(barrier, inc=1, device_id=where, device_id_type=MESH)
    pl.semaphore_wait(barrier, len(peers))

    parts = (
        (pk.at[0], 0, 128),
        (pv.at[0], 128, 128),
        (ck, 256, 64),
        (cv, 320, 64),
    )

    def kv_copies(j, chosen=range(4)):
        dzh, dy = j // NY, j % NY
        head = pl.multiple_of((lax.rem(zh + dzh, NZH) * NY + lax.rem(y + dy, NY)) * HD, HD)
        made = []
        for n in chosen:
            src, at, rows = parts[n]
            s = src.at[:, pl.ds(head, HD)]
            d = kv.at[j, c, pl.ds(at, rows), :]
            if j == 0:
                made.append(pltpu.make_async_copy(s, d, kv_loc.at[n]))
            else:
                made.append(remote(s, d, kv_send.at[j, n], kv_recv.at[j, n], (bulk, tp_at(dzh, dy, c))))
        return made

    for few in ((2, 3), (0,), (1,)):
        for j in (6, 5, 7, 4, 2, 1, 3, 0):
            for copy in kv_copies(j, few):
                copy.start()

    def w_copies(n):
        here = pltpu.make_async_copy(
            w.at[:, pl.ds(pl.multiple_of((2 * n + c) * FE, FE), FE)], wbuf.at[c, n], w_loc.at[n]
        )
        away = remote(
            w.at[:, pl.ds(pl.multiple_of((2 * n + oth) * FE, FE), FE)],
            wbuf.at[c, n],
            w_send.at[n],
            w_recv.at[n],
            (bulk, tp_at(0, 0, oth)),
        )
        return here, away

    for n in range(8):
        for copy in w_copies(n):
            copy.start()

    for n, known in enumerate(
        ([x_line[0], z_near[0]], x_line[:2], z_near, z_near, x_line)
    ):
        for where in known:
            pl.semaphore_signal(met.at[n], inc=1, device_id=where, device_id_type=MESH)
        pl.semaphore_wait(met.at[n], len(known))

    blk, nval = tables(lens, route, x, zl)
    tab[0:1, :] = blk
    tab[1:2, :] = nval
    t_copy = pltpu.make_async_copy(tab, order, t_sem)
    t_copy.start()
    q_copy.wait()
    r_copy.wait()
    t_copy.wait()

    def widen(i, carry):
        rows = pl.ds(pl.multiple_of(i * 64, 64), 64)
        at = pl.ds(i * 8, 8)
        qf[at] = qv[rows, :].astype(F32).reshape(8, 8, FE)
        rf[at] = rv[rows, :].astype(F32).reshape(8, 8, FE)
        return carry

    lax.fori_loop(0, 16, widen, 0)

    def own_part(j, core):
        dzh, dy = lax.div(j, NY), lax.rem(j, NY)
        i = (lax.rem(zh + NZH - dzh, NZH) * NY + lax.rem(y + NY - dy, NY)) * NC + core
        rows = pl.ds(pl.multiple_of(i * 64, 64), 64)
        at = pl.ds(i * 8, 8)
        qs = jnp.concatenate([qv[rows, h * HD : (h + 1) * HD] for h in range(LH)], axis=0)
        s = lax.dot_general(qs, kv[j, core, 256:320, :], NT, preferred_element_type=F32) * SCALE
        row = lax.broadcasted_iota(jnp.int32, s.shape, 0) & 63
        col = lax.broadcasted_iota(jnp.int32, s.shape, 1)
        s = jnp.where(col <= row, s, -1e30)
        m = jnp.max(s, axis=1, keepdims=True)
        e = jnp.exp2(s - m)
        total = jnp.sum(e, axis=1, keepdims=True)
        o = jnp.dot(e.astype(BF16), kv[j, core, 320:384, :], preferred_element_type=F32)
        m, total = jnp.broadcast_to(m, o.shape), jnp.broadcast_to(total, o.shape)
        for h in range(LH):
            cols = slice(h * HD, (h + 1) * HD)
            part = slice(h * 64, (h + 1) * 64)
            oown[at, :, cols] = o[part].reshape(8, 8, HD)
            mown[at, :, cols] = m[part].reshape(8, 8, HD)
            lown[at, :, cols] = total[part].reshape(8, 8, HD)

    pieces = ((256, 128, (2, 3)), (0, 128, (0,)), (128, 128, (1,)))

    def forward(j, n):
        part = kv.at[j, c, pl.ds(*pieces[n][:2]), :]
        return remote(part, part, fw_send.at[j, n], fw_recv.at[j, n], (bulk, tp_at(0, 0, oth)))

    def from_sibling(j, n):
        part = kv.at[j, oth, pl.ds(*pieces[n][:2]), :]
        return remote(part, part, fw_send.at[j, n], fw_recv.at[j, n], (bulk, tp_at(0, 0, oth)))

    def arrived(j, n):
        for copy in kv_copies(j, pieces[n][2]):
            if j == 0:
                copy.wait()
            else:
                copy.wait_recv()
        forward(j, n).start()

    near, late = (0, 1, 3, 2), (4, 5, 7, 6)
    for some in (near, late):
        for j in some:
            arrived(j, 0)
            own_part(j, c)
        for j in some:
            from_sibling(j, 0).wait_recv()
            own_part(j, oth)

    def all_here(n):
        for j in near + late:
            arrived(j, n)
        for j in near + late:
            from_sibling(j, n).wait_recv()

    def rows_of(k):
        return pl.ds(STARTS[k], CHUNKS[k])

    def attend(k, first=False):
        def gather(i, carry):
            b = order[0, STARTS[k] // BLK + i]
            n = order[1, STARTS[k] // BLK + i]
            at = pl.ds(pl.multiple_of(i * 8, 8), 8)
            qb, ob, mb, lb = qf[b], oown[b], mown[b], lown[b]
            for h in range(LH):
                cols = slice(h * HD, (h + 1) * HD)
                qc[h, at, :] = qb[:, cols]
                oc[h, at, :] = ob[:, cols]
                mc[h, at, :] = mb[:, cols]
                lc[h, at, :] = lb[:, cols]
            vc[at, :] = (lax.broadcasted_iota(jnp.int32, (8, HD), 0) < n).astype(F32)
            return carry

        lax.fori_loop(0, CHUNKS[k] // BLK, gather, 0)

        if first:
            all_here(1)
        size = CHUNKS[k]
        rows = LH * size
        qb = qc[:, :size].reshape(rows, HD).astype(BF16)
        top = None
        for j in range(8):
            s = lax.dot_general(
                qb, kv[j, :, 0:128, :].reshape(256, HD), NT, preferred_element_type=F32
            )
            scores[j, :rows] = s
            both = jnp.maximum(s[:, :HD], s[:, HD:])
            top = both if top is None else jnp.maximum(top, both)
        m_own = mc[:, :size].reshape(rows, HD)
        m = jnp.maximum(jnp.max(top, axis=1, keepdims=True) * SCALE, m_own)
        wide = jnp.concatenate([m, m], axis=1)
        if first:
            all_here(2)
        acc = jnp.zeros((rows, HD), F32)
        sums = jnp.zeros((rows, HD), F32)
        for j in range(8):
            e = jnp.exp2(scores[j, :rows] * SCALE - wide)
            sums = sums + (e[:, :HD] + e[:, HD:])
            acc = acc + jnp.dot(
                e.astype(BF16), kv[j, :, 128:256, :].reshape(256, HD), preferred_element_type=F32
            )
        a = jnp.exp2(m_own - m)
        total = jnp.sum(sums, axis=1, keepdims=True) + a * lc[:, :size].reshape(rows, HD)
        o = (acc + a * oc[:, :size].reshape(rows, HD)) / total
        good = vc[:size] > 0.5
        for h in range(LH):
            v = jnp.where(good, o[h * size : (h + 1) * size], 0.0)
            ctx[c, rows_of(k), h * HD : (h + 1) * HD] = v.astype(BF16)

    def ctx_copy(k, core):
        slot = ctx.at[core, rows_of(k)]
        return remote(slot, slot, c_send.at[k], c_recv.at[k], (bulk, tp_at(0, 0, oth)))

    def project(k, dy, dzh):
        n = lax.rem(zh + dzh, NZH) * NY + lax.rem(y + dy, NY)
        return jnp.dot(ctx[0, rows_of(k)], wbuf[0, n], preferred_element_type=F32) + jnp.dot(
            ctx[1, rows_of(k)], wbuf[1, n], preferred_element_type=F32
        )

    up, down = (bulk, tp_at(0, 1, c)), (bulk, tp_at(0, 3, c))
    toward = (up, down)

    def d2_copy(k, side):
        return remote(
            d2s.at[side, rows_of(k)], d2r.at[side, rows_of(k)], d2_send.at[k, side], d2_recv.at[k, side], toward[side]
        )

    def b_copy(k, side, dzh):
        return remote(
            bs.at[side, dzh, rows_of(k)],
            br.at[side, dzh, rows_of(k)],
            b_send.at[k, side, dzh],
            b_recv.at[k, side, dzh],
            toward[side],
        )

    def first_sends(k):
        ctx_copy(k, oth).wait_recv()
        for side in range(2):
            d2s[side, rows_of(k)] = project(k, 2, side).astype(BF16)
            d2_copy(k, side).start()
        for side in range(2):
            dzh = 1 - side
            bs[side, dzh, rows_of(k)] = project(k, 1 + 2 * side, dzh).astype(BF16)
            b_copy(k, side, dzh).start()

    def merged_sends(k):
        for side in range(2):
            mine = project(k, 1 + 2 * side, side)
            d2_copy(k, side).wait_recv()
            bs[side, side, rows_of(k)] = (mine + d2r[side, rows_of(k)].astype(F32)).astype(BF16)
            b_copy(k, side, side).start()

    mine32 = pl.ds(pl.multiple_of(bulk * 32, 32), 32)

    def x_copy(p, dzh):
        return remote(
            ds.at[dzh, pl.ds(p * SEND, SEND), :],
            out.at[dzh, mine32, :],
            x_send.at[p, dzh],
            x_recv.at[p, dzh],
            (bulk_at((p // NZL + 1) % NX, p % NZL), tp_at(dzh, 0, c)),
        )

    def stay():
        return pltpu.make_async_copy(ds.at[0, pl.ds(STAYS * SEND, SEND), :], out.at[0, mine32, :], q_sem)

    def x_half(k, dzh):
        places = range(STARTS[k] // SEND, (STARTS[k] + CHUNKS[k]) // SEND)
        return [x_copy(p, dzh) for p in places if dzh or p != STAYS]

    def finish(k):
        def gather(i, carry):
            b = order[0, STARTS[k] // BLK + i]
            n = order[1, STARTS[k] // BLK + i]
            row = lax.broadcasted_iota(jnp.int32, (8, FE), 0)
            rc[pl.ds(pl.multiple_of(i * 8, 8), 8), :] = jnp.where(row < n, rf[b], 0.0)
            return carry

        lax.fori_loop(0, CHUNKS[k] // BLK, gather, 0)
        for dzh in (1, 0):
            mine = project(k, 0, dzh)
            if dzh == 0:
                mine = mine + rc[: CHUNKS[k]]
            for side in (1 - dzh, dzh):
                b_copy(k, side, dzh).wait_recv()
                mine = mine + br[side, dzh, rows_of(k)].astype(F32)
            ds[dzh, rows_of(k)] = mine.astype(BF16)
            for copy in x_half(k, dzh):
                copy.start()
        if STARTS[k] <= STAYS * SEND < STARTS[k] + CHUNKS[k]:
            stay().start()

    def w_from_sibling(n):
        return remote(
            w.at[:, pl.ds(0, FE)], wbuf.at[oth, n], w_send.at[n], w_recv.at[n], (bulk, tp_at(0, 0, oth))
        )

    def weights(n, carry):
        pltpu.make_async_copy(w.at[:, pl.ds(0, FE)], wbuf.at[c, n], w_loc.at[n]).wait()
        w_from_sibling(n).wait_recv()
        return carry

    attend(0, first=True)
    ctx_copy(0, c).start()
    lax.fori_loop(0, 8, weights, 0)

    for k in range(NK + 1):
        if k > 0:
            merged_sends(k - 1)
        if k < NK:
            first_sends(k)
        if k < NK - 1:
            attend(k + 1)
            ctx_copy(k + 1, c).start()
        if k > 0:
            finish(k - 1)

    for k in range(NK):
        for dzh in range(NZH):
            for copy in x_half(k, dzh):
                copy.wait_recv()
    stay().wait()

    for j in range(1, 8):
        for copy in kv_copies(j):
            copy.wait_send()

    def left(n, carry):
        for part in range(3):
            forward(n, part).wait_send()
        w_from_sibling(n).wait_send()
        return carry

    lax.fori_loop(0, 8, left, 0)

    for k in range(NK):
        ctx_copy(k, c).wait_send()
        for side in range(2):
            d2_copy(k, side).wait_send()
            for dzh in range(NZH):
                b_copy(k, side, dzh).wait_send()
        for dzh in range(NZH):
            for copy in x_half(k, dzh):
                copy.wait_send()


def local(queries, comp_keys, comp_values, prefix_keys, prefix_values, lengths, routing, residual, out_weight):
    smem = pl.BlockSpec(memory_space=pltpu.SMEM)
    anywhere = pl.BlockSpec(memory_space=pl.ANY)
    vmem = pltpu.VMEM
    dma = pltpu.SemaphoreType.DMA
    both = pl.pallas_call(
        main_kernel,
        out_shape=pltpu.VMEM((NZH, 512, FE), BF16),
        in_specs=[smem, smem] + [anywhere] * 7,
        out_specs=pl.BlockSpec(memory_space=pltpu.VMEM),
        scratch_shapes=[
            vmem((8, 2, 384, HD), BF16),
            vmem((2, 8, 512, FE), BF16),
            vmem((1024, FE), BF16),
            vmem((1024, FE), BF16),
            vmem((128, 8, FE), F32),
            vmem((128, 8, FE), F32),
            vmem((128, 8, FE), F32),
            vmem((128, 8, FE), F32),
            vmem((128, 8, FE), F32),
            vmem((8, LH * CR, 256), F32),
            vmem((LH, CR, HD), F32),
            vmem((LH, CR, HD), F32),
            vmem((LH, CR, HD), F32),
            vmem((LH, CR, HD), F32),
            vmem((CR, HD), F32),
            vmem((CR, FE), F32),
            vmem((2, 512, FE), BF16),
            vmem((2, 512, FE), BF16),
            vmem((2, 512, FE), BF16),
            vmem((2, 2, 512, FE), BF16),
            vmem((2, 2, 512, FE), BF16),
            vmem((2, 512, FE), BF16),
            vmem((8, 128), jnp.int32),
            pltpu.SMEM((8, 128), jnp.int32),
            pltpu.SemaphoreType.REGULAR((5,)),
            dma,
            dma, dma, dma((4,)), dma((8, 4)), dma((8, 4)), dma((8, 3)), dma((8, 3)),
            dma((8,)), dma((8,)), dma((8,)),
            dma((NK,)), dma((NK,)), dma((NK, 2)), dma((NK, 2)), dma((NK, 2, 2)), dma((NK, 2, 2)),
            dma((ND, 2)), dma((ND, 2)),
        ],
        compiler_params=pltpu.CompilerParams(
            collective_id=0, has_side_effects=True, vmem_limit_bytes=56 * 2**20
        ),
        name="attend_project_send",
    )(lengths, routing, queries, comp_keys, comp_values, prefix_keys, prefix_values, residual, out_weight)
    return (both[0].astype(F32) + both[1].astype(F32)).astype(BF16)


def solution(mesh):
    return jax.shard_map(
        local,
        mesh=mesh,
        in_specs=(
            P("bulk", "tp"),
            P(("bulk", "tp"), None),
            P(("bulk", "tp"), None),
            P("bulk", "tp", None),
            P("bulk", "tp", None),
            P("bulk", None),
            P("bulk", None),
            P("bulk", "tp"),
            P("tp", None),
        ),
        out_specs=P("bulk", "tp"),
        check_vma=False,
    )
```

```python
import math

import jax
import jax.numpy as jnp
from jax import lax
from jax.experimental import pallas as pl
from jax.experimental.pallas import tpu as pltpu
from jax.sharding import PartitionSpec as P

HD = 128
BLK = 8
NX, NY, NZL, NZH, NC = 4, 4, 4, 2, 2
SEND = 32
CHUNKS = (96, 160, 160, 96)
NK = len(CHUNKS)
STARTS = tuple(sum(CHUNKS[:k]) for k in range(NK))
CR = max(CHUNKS)
ND = NX * NZL
STAYS = ND - NZL
LH = 4
FE = 512
SCALE = math.log2(math.e) / math.sqrt(HD)
F32, BF16 = jnp.float32, jnp.bfloat16
MESH = pl.DeviceIdType.MESH
NT = (((1,), (1,)), ((), ()))


def position():
    b, t = lax.axis_index("bulk"), lax.axis_index("tp")
    x, zl = lax.rem(b, NX), lax.div(b, NX)
    c, y, zh = lax.rem(t, NC), lax.rem(lax.div(t, NC), NY), lax.div(t, NC * NY)
    return x, zl, c, y, zh


def tables(lens, route, x, zl):
    sub = lax.broadcasted_iota(jnp.int32, (128, 128), 0)
    lane = lax.broadcasted_iota(jnp.int32, (128, 128), 1)
    size = jnp.zeros((128, 128), jnp.int32)
    for i in range(16):
        size = jnp.where((sub >> 3) == i, lens[0, i], size)
    first = (sub & 7) * BLK
    live = first < size
    one = jnp.where(live, 1, 0)
    rank = jnp.sum(jnp.where(sub < lane, one, 0), axis=0, keepdims=True)
    rank = jnp.sum(jnp.where(sub == lane, rank, 0), axis=1, keepdims=True)
    place = lax.broadcasted_iota(jnp.int32, (8, 128), 1)
    dest = jnp.full((8, 128), -1, jnp.int32)
    for j in range(64):
        dest = jnp.where(place == j, route[0, j], dest)
    dest = dest[0:1]
    down = jnp.sum(jnp.where(sub == lane, dest, 0), axis=1, keepdims=True)
    seen = jnp.sum(jnp.where((down == dest) & (sub < lane), 1, 0), axis=0, keepdims=True)
    k = ((dest & 3) - x + 2 * NX - 1) & 3
    dz = ((dest >> 2) - zl + NZL) & 3
    slot = (k * NZL + dz) * 4 + seen
    slot = jnp.sum(jnp.where((rank == lane) & live, slot, 0), axis=1, keepdims=True)
    here = (slot == lane) & live
    blk = jnp.sum(jnp.where(here, sub, 0), axis=0, keepdims=True)
    nval = jnp.sum(jnp.where(here, jnp.minimum(size - first, BLK), 0), axis=0, keepdims=True)
    return blk, nval


def main_kernel(
    lens, route, q, ck, cv, pk, pv, res, w, out,
    kv, wbuf, qv, rv, qf, rf, oown, mown, lown, scores, qc, oc, mc, lc, vc, rc,
    ctx, d2s, d2r, bs, br, ds, tab, order, met,
    t_sem, q_sem, r_sem, kv_loc, kv_send, kv_recv, fw_send, fw_recv, w_loc, w_send, w_recv,
    c_send, c_recv, d2_send, d2_recv, b_send, b_recv, x_send, x_recv,
):
    x, zl, c, y, zh = position()
    oth = 1 - c
    bulk = zl * NX + x

    def bulk_at(dx, dz):
        return lax.rem(zl + dz, NZL) * NX + lax.rem(x + dx, NX)

    def tp_at(dzh, dy, core):
        return (lax.rem(zh + dzh, NZH) * NY + lax.rem(y + dy, NY)) * NC + core

    def remote(src, dst, send, recv, where):
        return pltpu.make_async_remote_copy(
            src_ref=src, dst_ref=dst, send_sem=send, recv_sem=recv, device_id=where, device_id_type=MESH
        )

    q_copy = pltpu.make_async_copy(q, qv, q_sem)
    r_copy = pltpu.make_async_copy(res, rv, r_sem)
    q_copy.start()
    r_copy.start()

    barrier = pltpu.get_barrier_semaphore()
    peers = [(bulk, tp_at(dzh, dy, c)) for dzh in range(NZH) for dy in range(NY) if dzh or dy]
    peers += [(bulk, tp_at(0, 0, oth))]
    x_line = [(bulk_at(dx, 0), tp_at(0, 0, c)) for dx in (1, 3, 2)]
    z = zh * NZL + zl

    def z_at(dz):
        at = lax.rem(z + dz, NZH * NZL)
        return lax.rem(at, NZL) * NX + x, (lax.div(at, NZL) * NY + y) * NC + c

    z_near = [z_at(1), z_at(7)]
    peers += [x_line[1], z_near[1]]
    for where in peers:
        pl.semaphore_signal(barrier, inc=1, device_id=where, device_id_type=MESH)
    pl.semaphore_wait(barrier, len(peers))

    parts = (
        (pk.at[0], 0, 128),
        (pv.at[0], 128, 128),
        (ck, 256, 64),
        (cv, 320, 64),
    )

    def kv_copies(j, chosen=range(4)):
        dzh, dy = j // NY, j % NY
        head = pl.multiple_of((lax.rem(zh + dzh, NZH) * NY + lax.rem(y + dy, NY)) * HD, HD)
        made = []
        for n in chosen:
            src, at, rows = parts[n]
            s = src.at[:, pl.ds(head, HD)]
            d = kv.at[j, c, pl.ds(at, rows), :]
            if j == 0:
                made.append(pltpu.make_async_copy(s, d, kv_loc.at[n]))
            else:
                made.append(remote(s, d, kv_send.at[j, n], kv_recv.at[j, n], (bulk, tp_at(dzh, dy, c))))
        return made

    for few in ((2, 3), (0,), (1,)):
        for j in (6, 5, 7, 4, 2, 1, 3, 0):
            for copy in kv_copies(j, few):
                copy.start()

    def w_copies(n):
        here = pltpu.make_async_copy(
            w.at[:, pl.ds(pl.multiple_of((2 * n + c) * FE, FE), FE)], wbuf.at[c, n], w_loc.at[n]
        )
        away = remote(
            w.at[:, pl.ds(pl.multiple_of((2 * n + oth) * FE, FE), FE)],
            wbuf.at[c, n],
            w_send.at[n],
            w_recv.at[n],
            (bulk, tp_at(0, 0, oth)),
        )
        return here, away

    for n, known in enumerate(
        ([x_line[0], z_near[0]], x_line[:2], z_near, z_near, x_line)
    ):
        for where in known:
            pl.semaphore_signal(met.at[n], inc=1, device_id=where, device_id_type=MESH)
        pl.semaphore_wait(met.at[n], len(known))

    blk, nval = tables(lens, route, x, zl)
    tab[0:1, :] = blk
    tab[1:2, :] = nval
    t_copy = pltpu.make_async_copy(tab, order, t_sem)
    t_copy.start()
    for n in range(8):
        for copy in w_copies(n):
            copy.start()
    q_copy.wait()
    r_copy.wait()
    t_copy.wait()

    def widen(i, carry):
        rows = pl.ds(pl.multiple_of(i * 64, 64), 64)
        at = pl.ds(i * 8, 8)
        qf[at] = qv[rows, :].astype(F32).reshape(8, 8, FE)
        rf[at] = rv[rows, :].astype(F32).reshape(8, 8, FE)
        return carry

    lax.fori_loop(0, 16, widen, 0)

    def own_part(j, core):
        dzh, dy = lax.div(j, NY), lax.rem(j, NY)
        i = (lax.rem(zh + NZH - dzh, NZH) * NY + lax.rem(y + NY - dy, NY)) * NC + core
        rows = pl.ds(pl.multiple_of(i * 64, 64), 64)
        at = pl.ds(i * 8, 8)
        qs = jnp.concatenate([qv[rows, h * HD : (h + 1) * HD] for h in range(LH)], axis=0)
        s = lax.dot_general(qs, kv[j, core, 256:320, :], NT, preferred_element_type=F32) * SCALE
        row = lax.broadcasted_iota(jnp.int32, s.shape, 0) & 63
        col = lax.broadcasted_iota(jnp.int32, s.shape, 1)
        s = jnp.where(col <= row, s, -1e30)
        m = jnp.max(s, axis=1, keepdims=True)
        e = jnp.exp2(s - m)
        total = jnp.sum(e, axis=1, keepdims=True)
        o = jnp.dot(e.astype(BF16), kv[j, core, 320:384, :], preferred_element_type=F32)
        m, total = jnp.broadcast_to(m, o.shape), jnp.broadcast_to(total, o.shape)
        for h in range(LH):
            cols = slice(h * HD, (h + 1) * HD)
            part = slice(h * 64, (h + 1) * 64)
            oown[at, :, cols] = o[part].reshape(8, 8, HD)
            mown[at, :, cols] = m[part].reshape(8, 8, HD)
            lown[at, :, cols] = total[part].reshape(8, 8, HD)

    pieces = ((256, 128, (2, 3)), (0, 128, (0,)), (128, 128, (1,)))

    def forward(j, n):
        part = kv.at[j, c, pl.ds(*pieces[n][:2]), :]
        return remote(part, part, fw_send.at[j, n], fw_recv.at[j, n], (bulk, tp_at(0, 0, oth)))

    def from_sibling(j, n):
        part = kv.at[j, oth, pl.ds(*pieces[n][:2]), :]
        return remote(part, part, fw_send.at[j, n], fw_recv.at[j, n], (bulk, tp_at(0, 0, oth)))

    def arrived(j, n):
        for copy in kv_copies(j, pieces[n][2]):
            if j == 0:
                copy.wait()
            else:
                copy.wait_recv()
        forward(j, n).start()

    near, late = (0, 1, 3, 2), (4, 5, 7, 6)
    for some in (near, late):
        for j in some:
            arrived(j, 0)
            own_part(j, c)
        for j in some:
            from_sibling(j, 0).wait_recv()
            own_part(j, oth)

    def all_here(n):
        for j in near + late:
            arrived(j, n)
        for j in near + late:
            from_sibling(j, n).wait_recv()

    def rows_of(k):
        return pl.ds(STARTS[k], CHUNKS[k])

    def attend(k, first=False):
        def gather(i, carry):
            b = order[0, STARTS[k] // BLK + i]
            n = order[1, STARTS[k] // BLK + i]
            at = pl.ds(pl.multiple_of(i * 8, 8), 8)
            qb, ob, mb, lb = qf[b], oown[b], mown[b], lown[b]
            for h in range(LH):
                cols = slice(h * HD, (h + 1) * HD)
                qc[h, at, :] = qb[:, cols]
                oc[h, at, :] = ob[:, cols]
                mc[h, at, :] = mb[:, cols]
                lc[h, at, :] = lb[:, cols]
            vc[at, :] = (lax.broadcasted_iota(jnp.int32, (8, HD), 0) < n).astype(F32)
            return carry

        lax.fori_loop(0, CHUNKS[k] // BLK, gather, 0)

        if first:
            all_here(1)
        size = CHUNKS[k]
        rows = LH * size
        qb = qc[:, :size].reshape(rows, HD).astype(BF16)
        top = None
        for j in range(8):
            s = lax.dot_general(
                qb, kv[j, :, 0:128, :].reshape(256, HD), NT, preferred_element_type=F32
            )
            scores[j, :rows] = s
            both = jnp.maximum(s[:, :HD], s[:, HD:])
            top = both if top is None else jnp.maximum(top, both)
        m_own = mc[:, :size].reshape(rows, HD)
        m = jnp.maximum(jnp.max(top, axis=1, keepdims=True) * SCALE, m_own)
        wide = jnp.concatenate([m, m], axis=1)
        if first:
            all_here(2)
        acc = jnp.zeros((rows, HD), F32)
        sums = jnp.zeros((rows, HD), F32)
        for j in range(8):
            e = jnp.exp2(scores[j, :rows] * SCALE - wide)
            sums = sums + (e[:, :HD] + e[:, HD:])
            acc = acc + jnp.dot(
                e.astype(BF16), kv[j, :, 128:256, :].reshape(256, HD), preferred_element_type=F32
            )
        a = jnp.exp2(m_own - m)
        total = jnp.sum(sums, axis=1, keepdims=True) + a * lc[:, :size].reshape(rows, HD)
        o = (acc + a * oc[:, :size].reshape(rows, HD)) / total
        good = vc[:size] > 0.5
        for h in range(LH):
            v = jnp.where(good, o[h * size : (h + 1) * size], 0.0)
            ctx[c, rows_of(k), h * HD : (h + 1) * HD] = v.astype(BF16)

    def ctx_copy(k, core):
        slot = ctx.at[core, rows_of(k)]
        return remote(slot, slot, c_send.at[k], c_recv.at[k], (bulk, tp_at(0, 0, oth)))

    def project(k, dy, dzh):
        n = lax.rem(zh + dzh, NZH) * NY + lax.rem(y + dy, NY)
        return jnp.dot(ctx[0, rows_of(k)], wbuf[0, n], preferred_element_type=F32) + jnp.dot(
            ctx[1, rows_of(k)], wbuf[1, n], preferred_element_type=F32
        )

    up, down = (bulk, tp_at(0, 1, c)), (bulk, tp_at(0, 3, c))
    toward = (up, down)

    def d2_copy(k, side):
        return remote(
            d2s.at[side, rows_of(k)], d2r.at[side, rows_of(k)], d2_send.at[k, side], d2_recv.at[k, side], toward[side]
        )

    def b_copy(k, side, dzh):
        return remote(
            bs.at[side, dzh, rows_of(k)],
            br.at[side, dzh, rows_of(k)],
            b_send.at[k, side, dzh],
            b_recv.at[k, side, dzh],
            toward[side],
        )

    def first_sends(k):
        ctx_copy(k, oth).wait_recv()
        for side in range(2):
            d2s[side, rows_of(k)] = project(k, 2, side).astype(BF16)
            d2_copy(k, side).start()
        for side in range(2):
            dzh = 1 - side
            bs[side, dzh, rows_of(k)] = project(k, 1 + 2 * side, dzh).astype(BF16)
            b_copy(k, side, dzh).start()

    def merged_sends(k):
        for side in range(2):
            mine = project(k, 1 + 2 * side, side)
            d2_copy(k, side).wait_recv()
            bs[side, side, rows_of(k)] = (mine + d2r[side, rows_of(k)].astype(F32)).astype(BF16)
            b_copy(k, side, side).start()

    mine32 = pl.ds(pl.multiple_of(bulk * 32, 32), 32)

    def x_copy(p, dzh):
        return remote(
            ds.at[dzh, pl.ds(p * SEND, SEND), :],
            out.at[dzh, mine32, :],
            x_send.at[p, dzh],
            x_recv.at[p, dzh],
            (bulk_at((p // NZL + 1) % NX, p % NZL), tp_at(dzh, 0, c)),
        )

    def stay():
        return pltpu.make_async_copy(ds.at[0, pl.ds(STAYS * SEND, SEND), :], out.at[0, mine32, :], q_sem)

    def x_half(k, dzh):
        places = range(STARTS[k] // SEND, (STARTS[k] + CHUNKS[k]) // SEND)
        return [x_copy(p, dzh) for p in (places if dzh else places[::-1]) if dzh or p != STAYS]

    def finish(k):
        def gather(i, carry):
            b = order[0, STARTS[k] // BLK + i]
            n = order[1, STARTS[k] // BLK + i]
            row = lax.broadcasted_iota(jnp.int32, (8, FE), 0)
            rc[pl.ds(pl.multiple_of(i * 8, 8), 8), :] = jnp.where(row < n, rf[b], 0.0)
            return carry

        lax.fori_loop(0, CHUNKS[k] // BLK, gather, 0)
        for dzh in (1, 0):
            mine = project(k, 0, dzh)
            if dzh == 0:
                mine = mine + rc[: CHUNKS[k]]
            for side in (1 - dzh, dzh):
                b_copy(k, side, dzh).wait_recv()
                mine = mine + br[side, dzh, rows_of(k)].astype(F32)
            ds[dzh, rows_of(k)] = mine.astype(BF16)
            for copy in x_half(k, dzh):
                copy.start()
        if STARTS[k] <= STAYS * SEND < STARTS[k] + CHUNKS[k]:
            stay().start()

    def w_from_sibling(n):
        return remote(
            w.at[:, pl.ds(0, FE)], wbuf.at[oth, n], w_send.at[n], w_recv.at[n], (bulk, tp_at(0, 0, oth))
        )

    def weights(n, carry):
        pltpu.make_async_copy(w.at[:, pl.ds(0, FE)], wbuf.at[c, n], w_loc.at[n]).wait()
        w_from_sibling(n).wait_recv()
        return carry

    attend(0, first=True)
    ctx_copy(0, c).start()
    lax.fori_loop(0, 8, weights, 0)

    for k in range(NK + 1):
        if k > 0:
            merged_sends(k - 1)
        if k < NK:
            first_sends(k)
        if k < NK - 1:
            attend(k + 1)
            ctx_copy(k + 1, c).start()
        if k > 0:
            finish(k - 1)

    for k in range(NK):
        for dzh in range(NZH):
            for copy in x_half(k, dzh):
                copy.wait_recv()
    stay().wait()

    for j in range(1, 8):
        for copy in kv_copies(j):
            copy.wait_send()

    def left(n, carry):
        for part in range(3):
            forward(n, part).wait_send()
        w_from_sibling(n).wait_send()
        return carry

    lax.fori_loop(0, 8, left, 0)

    for k in range(NK):
        ctx_copy(k, c).wait_send()
        for side in range(2):
            d2_copy(k, side).wait_send()
            for dzh in range(NZH):
                b_copy(k, side, dzh).wait_send()
        for dzh in range(NZH):
            for copy in x_half(k, dzh):
                copy.wait_send()


def local(queries, comp_keys, comp_values, prefix_keys, prefix_values, lengths, routing, residual, out_weight):
    smem = pl.BlockSpec(memory_space=pltpu.SMEM)
    anywhere = pl.BlockSpec(memory_space=pl.ANY)
    vmem = pltpu.VMEM
    dma = pltpu.SemaphoreType.DMA
    both = pl.pallas_call(
        main_kernel,
        out_shape=pltpu.VMEM((NZH, 512, FE), BF16),
        in_specs=[smem, smem] + [anywhere] * 7,
        out_specs=pl.BlockSpec(memory_space=pltpu.VMEM),
        scratch_shapes=[
            vmem((8, 2, 384, HD), BF16),
            vmem((2, 8, 512, FE), BF16),
            vmem((1024, FE), BF16),
            vmem((1024, FE), BF16),
            vmem((128, 8, FE), F32),
            vmem((128, 8, FE), F32),
            vmem((128, 8, FE), F32),
            vmem((128, 8, FE), F32),
            vmem((128, 8, FE), F32),
            vmem((8, LH * CR, 256), F32),
            vmem((LH, CR, HD), F32),
            vmem((LH, CR, HD), F32),
            vmem((LH, CR, HD), F32),
            vmem((LH, CR, HD), F32),
            vmem((CR, HD), F32),
            vmem((CR, FE), F32),
            vmem((2, 512, FE), BF16),
            vmem((2, 512, FE), BF16),
            vmem((2, 512, FE), BF16),
            vmem((2, 2, 512, FE), BF16),
            vmem((2, 2, 512, FE), BF16),
            vmem((2, 512, FE), BF16),
            vmem((8, 128), jnp.int32),
            pltpu.SMEM((8, 128), jnp.int32),
            pltpu.SemaphoreType.REGULAR((5,)),
            dma,
            dma, dma, dma((4,)), dma((8, 4)), dma((8, 4)), dma((8, 3)), dma((8, 3)),
            dma((8,)), dma((8,)), dma((8,)),
            dma((NK,)), dma((NK,)), dma((NK, 2)), dma((NK, 2)), dma((NK, 2, 2)), dma((NK, 2, 2)),
            dma((ND, 2)), dma((ND, 2)),
        ],
        compiler_params=pltpu.CompilerParams(
            collective_id=0, has_side_effects=True, vmem_limit_bytes=56 * 2**20
        ),
        name="attend_project_send",
    )(lengths, routing, queries, comp_keys, comp_values, prefix_keys, prefix_values, residual, out_weight)
    return (both[0].astype(F32) + both[1].astype(F32)).astype(BF16)


def solution(mesh):
    return jax.shard_map(
        local,
        mesh=mesh,
        in_specs=(
            P("bulk", "tp"),
            P(("bulk", "tp"), None),
            P(("bulk", "tp"), None),
            P("bulk", "tp", None),
            P("bulk", "tp", None),
            P("bulk", None),
            P("bulk", None),
            P("bulk", "tp"),
            P("tp", None),
        ),
        out_specs=P("bulk", "tp"),
        check_vma=False,
    )
```
